128 devices in a mesh: rep: 32 (over z, y, core), tensor: 4 (over x).
Axes of the slice: x: 4, y: 4, z: 4, core: 2. Of those that a mesh axis runs over, the one named last changes fastest.
Arguments:
- hidden_in: bfloat16 [2048, 4096], P('rep', 'tensor'), may hold values from -25 to 25
- query: bfloat16 [2048, 4096], P('rep', 'tensor'), may hold values from -6 to 6
- new_kv: bfloat16 [2048, 2, 512], P('rep', None, 'tensor'), may hold values from -8 to 8
- pool: bfloat16 [4096, 128, 2, 512], P('rep', None, None, 'tensor'), may hold values from -8 to 8
- page_table: int32 [2048, 2], P('rep'), may hold values from 0 to 127, as said below
- lengths: int32 [2048], replicated, may hold values from 1 to 256, 262144 in all
- dest: int32 [32], replicated, may hold values from 0 to 31, each once
- out_weight: bfloat16 [4096, 4096], P('tensor'), may hold values from -0.1875 to 0.1875
- norm_gain: float32 [4096], P('tensor'), may hold values from 0.1 to 1.9
- gate_up: bfloat16 [4096, 2, 11008], P('tensor', None, 'rep'), may hold values from -0.09375 to 0.09375
- down_weight: bfloat16 [11008, 4096], P('rep', 'tensor'), may hold values from -0.109375 to 0.109375
Outputs:
- layer_out: bfloat16 [2048, 4096], P('rep', 'tensor')
The draws below stay inside these ranges and needn't reach their ends.
Inputs may be any that keep to these rules, and one draw needn't show every extreme that they name: `page_table`: within a group no two requests share a page.
All inputs are finite; a program needn't handle non-finite values.
Results may differ from the reference program's by a relative error of at most 0.03.
Values may be sent and summed in bfloat16 or wider, within the bound.
No kernel may reach another device: no remote copies, remote signals or barrier semaphores. Data moves between devices by JAX's collectives and lax.ppermute only.
A program may use at most 128 MiB of HBM per device.

```python
import math
import jax
import jax.numpy as jnp
import numpy as np
from jax import lax

D = 4096
H = 32
KVH = 4
HD = 128
FF = 11008
PAGE = 128
PPR = 2
R_DEV = 64
L_MAX = 256
NREQ = 2048
POOL = 4096
N_REP = 32


def page_rows(key):
    group_total = NREQ // R_DEV
    group_keys = jax.random.split(jax.random.fold_in(key, 7), group_total)
    perms = jax.vmap(lambda one_key: jax.random.permutation(one_key, R_DEV * PPR))(group_keys)
    return perms.reshape(NREQ, PPR).astype(jnp.int32)


def base_field(key, shape):
    return jax.random.truncated_normal(key, -4.0, 4.0, shape, jnp.float32)


def draw_page_table(key, part):
    return page_rows(key)


def draw_hidden_in(key, part):
    base = base_field(jax.random.fold_in(key, 31), (NREQ, D))
    trend = 3.0
    position = jnp.arange(D, dtype=jnp.float32) / (D - 1)
    column_scale = trend ** (position - 0.5) * jnp.exp(jax.random.uniform(jax.random.fold_in(key, 32), (D,), jnp.float32, -1.15, 1.15))
    row_scale = jnp.exp(jax.random.uniform(jax.random.fold_in(key, 33), (NREQ, 1), jnp.float32, -1.15, 1.15))
    return (0.35 * base * row_scale * column_scale[None, :]).astype(jnp.bfloat16)


def draw_query(key, part):
    base = base_field(jax.random.fold_in(key, 21), (NREQ, H, HD))
    return base.reshape(NREQ, H * HD).astype(jnp.bfloat16)


def draw_new_kv(key, part):
    key_part = base_field(jax.random.fold_in(key, 41), (NREQ, KVH, HD))
    value_part = 2.0 * base_field(jax.random.fold_in(key, 42), (NREQ, KVH, HD))
    stacked = jnp.stack([key_part.reshape(NREQ, KVH * HD), value_part.reshape(NREQ, KVH * HD)], axis=1)
    return stacked.astype(jnp.bfloat16)


def draw_pool(key, part):
    key_part = base_field(jax.random.fold_in(key, 51), (POOL, PAGE, KVH * HD))
    value_part = 2.0 * base_field(jax.random.fold_in(key, 52), (POOL, PAGE, KVH * HD))
    return jnp.stack([key_part, value_part], axis=2).astype(jnp.bfloat16)


def block_levels(key, shape, shards, smallest, high):
    loudness = 1.0
    for dim, shards_of in shards:
        steps = jax.random.uniform(jax.random.fold_in(jax.random.fold_in(key, 6), dim), (shards_of,), jnp.float32, smallest / len(shards), high / len(shards))
        loudness = loudness * jnp.repeat(jnp.exp(steps), shape[dim] // shards_of).reshape((-1,) + (1,) * (len(shape) - 1 - dim))
    return loudness


def profile(number_of, total, limit, slope):
    loads = [(1 << 20) // math.isqrt(grade ** slope) + 1 for grade in range(2, number_of + 1)]
    spare, given = total - limit - (number_of - 1), [1] * (number_of - 1)
    while spare > 0:
        free = [i for i in range(number_of - 1) if given[i] < limit]
        whole, left = sum([loads[i] for i in free]), spare
        for i in free:
            extra = min(limit - given[i], max(1, left * loads[i] // whole), spare)
            given[i] = given[i] + extra
            spare = spare - extra
    return np.array([limit] + given)


def uneven(rng, number_of, total, bound, skew):
    if number_of == 2:
        one = jax.random.randint(rng, (), max(1, total - bound), min(bound, total - 1) + 1)
        return jnp.stack([one, total - one])
    sizes = jnp.asarray(profile(number_of, total, bound, skew), jnp.int32)
    twos = (number_of - 1) // 2
    giver, sink = sizes[1:1 + 2 * twos:2], sizes[2:2 + 2 * twos:2]
    margin = jnp.minimum(giver - 1, bound - sink)
    passed = jax.random.randint(jax.random.fold_in(rng, 1), (twos,), 0, 1 << 20) % (margin + 1)
    sizes = sizes.at[1:1 + 2 * twos:2].set(giver - passed).at[2:2 + 2 * twos:2].set(sink + passed)
    return sizes[jax.random.permutation(jax.random.fold_in(rng, 2), number_of)]


def bell_draw(key, extent, deviation, limit, cuts=(), held_as=jnp.bfloat16):
    level = block_levels(key, extent, cuts, -0.22, 0.18) if cuts else 1.0
    result = jax.random.normal(key, extent, jnp.float32) * deviation * level
    return jnp.minimum(jnp.maximum(result, -limit), limit).astype(held_as)


def setup_inputs(seed: int = 0) -> dict:
    keys = jax.random.split(jax.random.key(seed), 12)
    return {
        "hidden_in": draw_hidden_in(jax.random.fold_in(keys[11], 71), 0),
        "query": draw_query(jax.random.fold_in(keys[11], 71), 0),
        "new_kv": draw_new_kv(jax.random.fold_in(keys[11], 71), 0),
        "pool": draw_pool(jax.random.fold_in(keys[11], 71), 0),
        "page_table": draw_page_table(jax.random.fold_in(keys[11], 71), 0),
        "lengths": uneven(keys[5], NREQ, NREQ * L_MAX // 2, L_MAX, 2).astype(jnp.int32),
        "dest": jax.random.permutation(keys[6], N_REP).astype(jnp.int32),
        "out_weight": bell_draw(keys[7], (H * HD, D), (H * HD // 4) ** -0.5, 0.1875, ((0, 4),)),
        "norm_gain": jnp.clip(1.0 + 0.18 * jax.random.normal(keys[8], (D,), jnp.float32), 0.1, 1.9),
        "gate_up": bell_draw(keys[9], (D, 2, FF), D ** -0.5, 0.09375, ((0, 4), (2, 32))),
        "down_weight": bell_draw(keys[10], (FF, D), (FF // 4) ** -0.5, 0.109375, ((0, 32), (1, 4))),
    }


EPSILON = 1e-05

def attend(queries, cache_block, new_pair, counts):
    row_count = cache_block.shape[0]
    cache_len = cache_block.shape[1]
    group_size = H // KVH
    query_heads = queries.astype(jnp.float32).reshape(row_count, KVH, group_size, HD)
    key_heads = cache_block[:, :, 0].astype(jnp.float32).reshape(row_count, cache_len, KVH, HD)
    value_heads = cache_block[:, :, 1].astype(jnp.float32).reshape(row_count, cache_len, KVH, HD)
    new_key = new_pair[:, 0].astype(jnp.float32).reshape(row_count, KVH, HD)
    new_value = new_pair[:, 1].astype(jnp.float32).reshape(row_count, KVH, HD)
    score_scale = HD ** (-0.5)
    scores = jnp.einsum('nkgd,nlkd->nkgl', query_heads, key_heads) * score_scale
    own_score = jnp.einsum('nkgd,nkd->nkg', query_heads, new_key) * score_scale
    in_range = (jnp.arange(cache_len, dtype=jnp.int32)[None, :] < counts[:, None])[:, None, None, :]
    masked = jnp.where(in_range, scores, -jnp.inf)
    peak_score = jnp.maximum(lax.optimization_barrier(jnp.max(masked, axis=-1)), own_score)
    weights = jnp.where(in_range, jnp.exp(scores - peak_score[..., None]), 0.0)
    own_weight = jnp.exp(own_score - peak_score)
    denominator = lax.optimization_barrier(jnp.sum(weights, axis=-1)) + own_weight
    weights_b = lax.optimization_barrier(weights.astype(jnp.bfloat16)).astype(jnp.float32)
    own_b = lax.optimization_barrier(own_weight.astype(jnp.bfloat16)).astype(jnp.float32)
    weighted = jnp.einsum('nkgl,nlkd->nkgd', weights_b, value_heads)
    weighted = weighted + jnp.einsum('nkg,nkd->nkgd', own_b, new_value)
    return (weighted / denominator[..., None]).astype(jnp.bfloat16).reshape(row_count, H * HD)

def reference(hidden_in, query, new_kv, pool, page_table, lengths, dest, out_weight, norm_gain, gate_up, down_weight):
    request_ids = jnp.arange(NREQ, dtype=jnp.int32)
    group_of = request_ids // R_DEV
    global_pages = page_table + (group_of * (R_DEV * PPR))[:, None]

    def one_group(index):
        start = (index * R_DEV).astype(jnp.int32)
        table_rows = lax.dynamic_slice_in_dim(global_pages, start, R_DEV)
        cache_block = pool[table_rows].reshape(R_DEV, L_MAX, 2, KVH * HD)
        return attend(lax.dynamic_slice_in_dim(query, start, R_DEV), cache_block, lax.dynamic_slice_in_dim(new_kv, start, R_DEV), lax.dynamic_slice_in_dim(lengths, start, R_DEV))
    attention = lax.map(one_group, jnp.arange(N_REP, dtype=jnp.int32)).reshape(NREQ, H * HD)
    inverse = jnp.zeros((N_REP,), jnp.int32).at[dest].set(jnp.arange(N_REP, dtype=jnp.int32))
    slot_of = request_ids % R_DEV
    order = jnp.where(slot_of == R_DEV - 1, inverse[group_of] * R_DEV + slot_of, request_ids).astype(jnp.int32)
    served_hidden = hidden_in[order]
    served_attention = attention[order]
    residual = served_hidden.astype(jnp.float32) + jnp.dot(served_attention, out_weight, preferred_element_type=jnp.float32)
    mean_square = lax.optimization_barrier(jnp.mean(residual * residual, axis=1, keepdims=True))
    normed = (residual * lax.rsqrt(mean_square + EPSILON) * norm_gain[None, :]).astype(jnp.bfloat16)
    both = jnp.dot(normed, gate_up.reshape(D, 2 * FF), preferred_element_type=jnp.float32)
    gate = both[:, :FF]
    up_part = both[:, FF:]
    activated = (jax.nn.silu(gate) * up_part).astype(jnp.bfloat16)
    block_units = FF // N_REP
    act_blocks = activated.reshape(NREQ, N_REP, block_units)
    down_blocks = down_weight.reshape(N_REP, block_units, D)

    def add_block(total, index):
        piece = jnp.dot(act_blocks[:, index], down_blocks[index], preferred_element_type=jnp.float32)
        rounded = lax.optimization_barrier(piece.astype(jnp.bfloat16)).astype(jnp.float32)
        return (total + rounded, None)
    mixed, unused = lax.scan(add_block, jnp.zeros((NREQ, D), jnp.float32), jnp.arange(N_REP, dtype=jnp.int32))
    return (residual + mixed).astype(jnp.bfloat16)
```

```python
import jax
import jax.numpy as jnp
from jax import lax
from jax.sharding import Mesh, PartitionSpec as P

D = 4096
HD = 128
EPSILON = 1e-05
REP = ("z", "y", "c")
SIDE = 4


def x_ring(shift):
    return [(i, (i + shift) % SIDE) for i in range(SIDE)]


def chip_ring(shift, first):
    pairs = []
    for z in range(SIDE):
        for y in range(SIDE):
            for c in range(2):
                if (c == 0) == first:
                    to = (((z + shift) % SIDE) * SIDE + y) * 2 + c
                else:
                    to = (z * SIDE + (y + shift) % SIDE) * 2 + c
                pairs.append(((z * SIDE + y) * 2 + c, to))
    return pairs


def along_x(value, shift):
    return lax.ppermute(value, "x", x_ring(shift))


def along_chips(value, shift, first):
    return lax.ppermute(value, REP, chip_ring(shift, first))


def other_core(value):
    return lax.ppermute(value, "c", [(0, 1), (1, 0)])


def attend(queries, cache_block, new_pair, counts):
    row_count = cache_block.shape[0]
    cache_len = cache_block.shape[1]
    kv_width = cache_block.shape[3]
    kv_heads = kv_width // HD
    group_size = queries.shape[1] // kv_width
    query_heads = queries.reshape(row_count, kv_heads, group_size, HD)
    key_heads = cache_block[:, :, 0].reshape(row_count, cache_len, kv_heads, HD)
    value_heads = cache_block[:, :, 1].reshape(row_count, cache_len, kv_heads, HD)
    new_key = new_pair[:, 0].reshape(row_count, kv_heads, HD)
    new_value = new_pair[:, 1].reshape(row_count, kv_heads, HD)
    score_scale = HD ** (-0.5)
    scores = (
        jnp.einsum("nkgd,nlkd->nkgl", query_heads, key_heads, preferred_element_type=jnp.float32)
        * score_scale
    )
    own_score = (
        jnp.einsum("nkgd,nkd->nkg", query_heads, new_key, preferred_element_type=jnp.float32)
        * score_scale
    )
    in_range = (jnp.arange(cache_len, dtype=jnp.int32)[None, :] < counts[:, None])[:, None, None, :]
    masked = jnp.where(in_range, scores, -jnp.inf)
    peak_score = jnp.maximum(jnp.max(masked, axis=-1), own_score)
    weights = jnp.where(in_range, jnp.exp(scores - peak_score[..., None]), 0.0)
    own_weight = jnp.exp(own_score - peak_score)
    denominator = jnp.sum(weights, axis=-1) + own_weight
    weighted = jnp.einsum(
        "nkgl,nlkd->nkgd",
        weights.astype(jnp.bfloat16),
        value_heads,
        preferred_element_type=jnp.float32,
    )
    weighted = weighted + jnp.einsum(
        "nkg,nkd->nkgd",
        own_weight.astype(jnp.bfloat16),
        new_value,
        preferred_element_type=jnp.float32,
    )
    return (weighted / denominator[..., None]).astype(jnp.bfloat16).reshape(row_count, -1)


def slot_sources(dest):
    z, y, c = (lax.axis_index(a) for a in REP)
    other, second, first = jnp.meshgrid(
        jnp.arange(2), jnp.arange(SIDE), jnp.arange(SIDE), indexing="ij"
    )
    core = (c + other) % 2
    slot_z = (z - jnp.where(core == 0, first, second)) % SIDE
    slot_y = (y - jnp.where(core == 0, second, first)) % SIDE
    group = ((slot_z * SIDE + slot_y) * 2 + core).reshape(-1)
    target = jnp.sum(
        jnp.where(group[:, None] == jnp.arange(dest.shape[0])[None, :], dest[None, :], 0), axis=1
    )
    hit = group[:, None] == target[None, :]
    return jnp.sum(jnp.where(hit, jnp.arange(group.shape[0])[None, :], 0), axis=1)


def local(
    hidden_in,
    query,
    new_kv,
    pool,
    page_table,
    lengths,
    dest,
    out_weight,
    norm_gain,
    gate_up,
    down_weight,
):
    rows_here = hidden_in.shape[0]
    block = rows_here // SIDE
    x = lax.axis_index("x")
    my_group = lax.axis_index(REP)
    units = gate_up.shape[2]
    width = gate_up.shape[0]

    gate_up_t = jnp.transpose(gate_up, (1, 2, 0)).reshape(2 * units, width)
    weights = lax.all_gather(gate_up_t, "x", axis=0, tiled=False)
    gains = jnp.stack([norm_gain] + [along_x(norm_gain, s) for s in range(1, SIDE)])
    gain = gains[(x - jnp.arange(SIDE)) % SIDE].reshape(-1)

    cache_rows = pool[page_table].reshape(rows_here, -1, 2, pool.shape[3])
    my_lengths = lax.dynamic_slice_in_dim(lengths, my_group * rows_here, rows_here)
    attention = attend(query, cache_rows, new_kv, my_lengths)
    projected = jnp.dot(attention, out_weight, preferred_element_type=jnp.float32)
    mine = (jnp.arange(SIDE) == x)[None, :, None]
    projected = projected.reshape(rows_here, SIDE, width) + jnp.where(
        mine, hidden_in.astype(jnp.float32)[:, None, :], 0.0
    )
    projected = projected.astype(jnp.bfloat16).reshape(SIDE, block, SIDE * width)

    def for_shift(s):
        return lax.dynamic_index_in_dim(projected, (x + s) % SIDE, 0, keepdims=False)

    parts = [for_shift(0)] + [along_x(for_shift(s), s) for s in (1, 3, 2)]
    residual = sum(p.astype(jnp.float32) for p in parts)
    square = jnp.mean(residual * residual, axis=1, keepdims=True)
    normed = (residual * lax.rsqrt(square + EPSILON) * gain[None, :]).astype(jnp.bfloat16)

    residual_b = residual.astype(jnp.bfloat16).reshape(block, SIDE, width)

    def piece(s):
        return lax.dynamic_index_in_dim(residual_b, (x + s) % SIDE, 1, keepdims=False)

    pieces = jnp.stack([piece(0)] + [along_x(piece(s), s) for s in range(1, SIDE)])
    home = pieces[(x - jnp.arange(SIDE)) % SIDE].reshape(rows_here, width)

    first = jnp.concatenate([normed] + [along_chips(normed, s, True) for s in (1, 2, 3)])
    second = [first] + [along_chips(first, s, False) for s in (1, 2, 3)]
    every = jnp.concatenate(second + [other_core(v) for v in second])

    both = sum(
        lax.dot_general(
            every[:, t * width : (t + 1) * width],
            weights[t],
            (((1,), (1,)), ((), ())),
            preferred_element_type=jnp.float32,
        )
        for t in range(SIDE)
    )
    activated = jax.nn.silu(both[:, :units]) * both[:, units:]
    source = slot_sources(dest)
    slots = source.shape[0]
    source = jnp.where(x == SIDE - 1, source, jnp.arange(slots))
    activated = activated.astype(jnp.bfloat16).reshape(slots, block, units)
    last = activated[source, block - 1]
    activated = jnp.concatenate([activated[:, : block - 1], last[:, None]], axis=1)

    gathered = jnp.stack([activated] + [along_x(activated, s) for s in range(1, SIDE)])
    gathered = gathered[(x - jnp.arange(SIDE)) % SIDE]
    gathered = jnp.transpose(gathered, (1, 0, 2, 3)).reshape(slots * rows_here, units)
    down = jnp.dot(gathered, down_weight, preferred_element_type=jnp.float32)
    down = down.reshape(slots, rows_here, width)
    moved_to = slot_sources_inverse(dest)
    row = jnp.arange(rows_here)[None, :]
    target = jnp.where(row == rows_here - 1, moved_to, 0)
    mine = (jnp.arange(slots)[:, None] == target)[..., None]
    down = down + jnp.where(mine, home.astype(jnp.float32)[None], 0.0)
    down = down.astype(jnp.bfloat16).reshape(2, SIDE, SIDE * rows_here, width)

    summed = [
        (down[0, s].astype(jnp.float32) + other_core(down[1, s]).astype(jnp.float32)).astype(
            jnp.bfloat16
        )
        for s in range(SIDE)
    ]
    back = [summed[0]] + [along_chips(summed[s], -s, False) for s in (1, 2, 3)]
    total = sum(v.astype(jnp.float32) for v in back).astype(jnp.bfloat16)
    total = total.reshape(SIDE, rows_here, width)
    back = [total[0]] + [along_chips(total[s], -s, True) for s in (1, 2, 3)]
    return sum(v.astype(jnp.float32) for v in back).astype(jnp.bfloat16)


def slot_sources_inverse(dest):
    source = slot_sources(dest)
    return jnp.sum(jnp.where(source == 0, jnp.arange(source.shape[0]), 0))


def solution(mesh):
    chips = Mesh(mesh.devices.reshape(SIDE, SIDE, 2, SIDE), ("z", "y", "c", "x"))
    return jax.shard_map(
        local,
        mesh=chips,
        in_specs=(
            P(REP, "x"),
            P(REP, "x"),
            P(REP, None, "x"),
            P(REP, None, None, "x"),
            P(REP, None),
            P(),
            P(),
            P("x", None),
            P("x"),
            P("x", None, REP),
            P(REP, "x"),
        ),
        out_specs=P(REP, "x"),
        check_vma=False,
    )
```

```python
import jax
import jax.numpy as jnp
from jax import lax
from jax.experimental import pallas as pl
from jax.experimental.pallas import tpu as pltpu
from jax.sharding import Mesh, PartitionSpec as P

HD = 128
EPSILON = 1e-05
REP = ("z", "y", "c")
SIDE = 4
CHUNKS = 8
HBM = pl.BlockSpec(memory_space=pltpu.HBM)
VM = pl.BlockSpec(memory_space=pltpu.VMEM)
SM = pl.BlockSpec(memory_space=pltpu.SMEM)


def params(megabytes):
    return pltpu.CompilerParams(vmem_limit_bytes=megabytes * 1024 * 1024)


def in_hbm(value):
    return pltpu.with_memory_space_constraint(value, pltpu.HBM)


def x_ring(shift):
    return [(i, (i + shift) % SIDE) for i in range(SIDE)]


def chip_ring(shift, first):
    pairs = []
    for z in range(SIDE):
        for y in range(SIDE):
            for c in range(2):
                if (c == 0) == first:
                    to = (((z + shift) % SIDE) * SIDE + y) * 2 + c
                else:
                    to = (z * SIDE + (y + shift) % SIDE) * 2 + c
                pairs.append(((z * SIDE + y) * 2 + c, to))
    return pairs


def along_x(value, shift):
    return lax.ppermute(value, "x", x_ring(shift))


def along_chips(value, shift, first):
    return lax.ppermute(value, REP, chip_ring(shift, first))


def other_core(value):
    return lax.ppermute(value, "c", [(0, 1), (1, 0)])


def attend_kernel(table, lengths, place, query, new_kv, hidden, gain, pool, weight, *refs):
    outs = refs[:SIDE]
    pages, weights, queries, pairs, homes, gains, by_head, heads, rows, page_sem, weight_sem, sem = refs[
        SIDE:
    ]
    page_rows = pool.shape[1]
    span_rows = 2 * page_rows
    requests, width = hidden.shape
    group = width // HD
    block = requests // SIDE
    many = HD // group
    scale = HD ** (-0.5)
    share = pool.shape[0] // CHUNKS
    x = place[0]
    home = place[1] * requests

    def page_copy(n):
        part = pl.ds(n * share, share)
        return pltpu.make_async_copy(pool.at[part], pages.at[part], page_sem.at[n])

    def weight_copy(n):
        return pltpu.make_async_copy(
            weight.at[:, pl.ds(n * width, width)], weights.at[n], weight_sem.at[n]
        )

    small = [
        pltpu.make_async_copy(source, into, sem.at[n])
        for n, (source, into) in enumerate(
            ((query, queries), (new_kv, pairs), (hidden, homes), (gain, gains))
        )
    ]
    for copy in small:
        copy.start()
    for n in range(CHUNKS):
        page_copy(n).start()
    for n in range(SIDE):
        weight_copy(n).start()
    for copy in small:
        copy.wait()

    row = lax.broadcasted_iota(jnp.int32, (span_rows, HD), 0)
    is_key = row % 2 == 0
    position = row // 2
    owner = lax.broadcasted_iota(jnp.int32, (HD, HD), 1) // group
    lane = lax.broadcasted_iota(jnp.int32, (1, HD), 1) // group

    def one_group(g):
        r0 = g * many
        for h in range(group):
            by_head[g, pl.ds(h, many, stride=group), :] = queries[
                r0 : r0 + many, h * HD : (h + 1) * HD
            ].astype(jnp.float32)
        q_t = jnp.transpose(by_head[g])
        sides = jnp.concatenate(
            [jnp.where(owner == i, q_t, 0.0).astype(jnp.bfloat16) for i in range(many)], axis=0
        )
        span = jnp.zeros((1, HD), jnp.int32)
        for i in range(many):
            span = jnp.where(lane == i, lengths[home + r0 + i], span)
        if g == 0:
            for n in range(CHUNKS):
                page_copy(n).wait()

        def both(i):
            r = r0 + i
            return jnp.concatenate([pages[table[0, r]], pages[table[1, r]]], axis=0)

        cached = jnp.concatenate([both(i) for i in range(many)], axis=1)
        scores = jnp.dot(cached, sides, preferred_element_type=jnp.float32) * scale
        fresh = [pairs[r0 + i].astype(jnp.float32) for i in range(many)]
        own = jnp.dot(
            jnp.concatenate(fresh, axis=1).astype(jnp.bfloat16),
            sides,
            preferred_element_type=jnp.float32,
        )[0:1] * scale
        valid = is_key & (position < span)
        peak = jnp.maximum(
            jnp.max(jnp.where(valid, scores, -jnp.inf), axis=0, keepdims=True), own
        )
        w = jnp.where(valid, jnp.exp(scores - peak), 0.0)
        w_own = jnp.exp(own - peak)
        total = jnp.sum(w, axis=0, keepdims=True) + w_own
        line = lax.broadcasted_iota(jnp.int32, (HD, HD), 0)
        w = jnp.transpose(pltpu.roll(w, 1, 0))
        last = jnp.transpose(jnp.where(line == 0, w_own, total))
        w_own = last[:, 0:1].astype(jnp.bfloat16).astype(jnp.float32)
        total = last[:, 1:2]
        for i in range(many):
            at = slice(i * group, (i + 1) * group)
            mixed = jnp.dot(w[at].astype(jnp.bfloat16), both(i), preferred_element_type=jnp.float32)
            heads[pl.ds((r0 + i) * group, group), :] = (mixed + w_own[at] * fresh[i][1:2]) / total[at]

    for g in range(requests // many):
        one_group(g)
    attention = jnp.concatenate(
        [heads[pl.ds(h, requests, stride=group), :].astype(jnp.bfloat16) for h in range(group)],
        axis=1,
    )
    for n in range(SIDE):
        weight_copy(n).wait()
        part = jnp.dot(attention, weights[n], preferred_element_type=jnp.float32)
        part = part + jnp.where(x == n, homes[...].astype(jnp.float32), 0.0)
        part = part.astype(jnp.bfloat16)
        for t in range(SIDE):
            rows[t, :, n * width : (n + 1) * width] = part[t * block : (t + 1) * block]
    high = gains[...].astype(jnp.bfloat16).astype(jnp.float32)
    extra = jnp.concatenate([high, gains[...] - high], axis=0).astype(jnp.bfloat16)
    for s in range(SIDE):
        outs[s][:, : SIDE * width] = rows[(x + s) % SIDE]
        outs[s][:, SIDE * width :] = extra


def attend_project(table, lengths, place, query, new_kv, hidden, gain, pool, weight):
    requests, width = hidden.shape
    block = requests // SIDE
    group = width // HD
    groups = requests * group // HD
    page_rows = pool.shape[1] * pool.shape[2]
    out = jax.ShapeDtypeStruct((block, SIDE * width + HD), jnp.bfloat16)
    return pl.pallas_call(
        attend_kernel,
        out_shape=[out] * SIDE,
        in_specs=[SM, SM, SM] + [HBM] * 6,
        out_specs=[VM] * SIDE,
        scratch_shapes=[
            pltpu.VMEM((pool.shape[0], page_rows, HD), jnp.bfloat16),
            pltpu.VMEM((SIDE, weight.shape[0], width), jnp.bfloat16),
            pltpu.VMEM(query.shape, jnp.bfloat16),
            pltpu.VMEM(new_kv.shape, jnp.bfloat16),
            pltpu.VMEM(hidden.shape, jnp.bfloat16),
            pltpu.VMEM((group, HD), jnp.float32),
            pltpu.VMEM((groups, HD, HD), jnp.float32),
            pltpu.VMEM((requests * group, HD), jnp.float32),
            pltpu.VMEM((SIDE, block, SIDE * width), jnp.bfloat16),
            pltpu.SemaphoreType.DMA((CHUNKS,)),
            pltpu.SemaphoreType.DMA((SIDE,)),
            pltpu.SemaphoreType.DMA((4,)),
        ],
        compiler_params=params(36),
        name="attend_project",
    )(
        table,
        lengths,
        place,
        in_hbm(query),
        in_hbm(new_kv),
        in_hbm(hidden),
        in_hbm(gain.reshape(group, HD)),
        in_hbm(pool.reshape(pool.shape[0], page_rows, HD)),
        in_hbm(weight),
    )


def norm_kernel(place, *refs):
    parts, (normed, *pieces, gains, kept) = refs[:SIDE], refs[SIDE:]
    x = place[0]
    width = kept.shape[2]
    lines = width // HD
    for s in range(SIDE):
        extra = parts[s][:, SIDE * width :].astype(jnp.float32)
        gains[(x + SIDE - s) % SIDE] = extra[:lines] + extra[lines:]
    square = 0.0
    residual = []
    for n in range(SIDE):
        at = slice(n * width, (n + 1) * width)
        value = sum(p[:, at].astype(jnp.float32) for p in parts)
        square = square + jnp.sum(value * value, axis=1, keepdims=True)
        kept[n] = value.astype(jnp.bfloat16)
        residual.append(value)
    factor = lax.rsqrt(square / (SIDE * width) + EPSILON)
    for n in range(SIDE):
        gain = gains[n]
        for j in range(lines):
            value = residual[n][:, j * HD : (j + 1) * HD] * factor * gain[j : j + 1]
            normed[:, n * width + j * HD : n * width + (j + 1) * HD] = value.astype(jnp.bfloat16)
    for s in range(SIDE):
        pieces[s][...] = kept[(x + s) % SIDE]


def normalise(place, parts, width):
    block = parts[0].shape[0]
    piece = jax.ShapeDtypeStruct((block, width), jnp.bfloat16)
    return pl.pallas_call(
        norm_kernel,
        out_shape=[jax.ShapeDtypeStruct((block, SIDE * width), jnp.bfloat16)] + [piece] * SIDE,
        in_specs=[SM] + [VM] * SIDE,
        out_specs=[VM] * (SIDE + 1),
        scratch_shapes=[
            pltpu.VMEM((SIDE, width // HD, HD), jnp.float32),
            pltpu.VMEM((SIDE, block, width), jnp.bfloat16),
        ],
        compiler_params=params(16),
        name="normalise",
    )(place, *parts)


def join_kernel(*refs):
    parts, out = refs[:-1], refs[-1]
    rows = parts[0].shape[0]
    for i, part in enumerate(parts):
        out[i * rows : (i + 1) * rows] = part[...]


def join(parts):
    rows, width = parts[0].shape
    return pl.pallas_call(
        join_kernel,
        out_shape=jax.ShapeDtypeStruct((len(parts) * rows, width), parts[0].dtype),
        in_specs=[VM] * len(parts),
        out_specs=VM,
        compiler_params=params(4),
        name="join",
    )(*parts)


def split_kernel(both, gate, up, sem):
    copies = [
        pltpu.make_async_copy(both.at[k], into, sem.at[k]) for k, into in enumerate((gate, up))
    ]
    for c in copies:
        c.start()
    for c in copies:
        c.wait()


def split(both):
    half = jax.ShapeDtypeStruct(both.shape[1:], both.dtype)
    return pl.pallas_call(
        split_kernel,
        out_shape=[half, half],
        in_specs=[HBM],
        out_specs=[VM, VM],
        scratch_shapes=[pltpu.SemaphoreType.DMA((2,))],
        compiler_params=params(4),
        name="split",
    )(in_hbm(both))


def gate_up_kernel(place, source, *refs):
    blocks, sides, out = refs[: 2 * SIDE], refs[2 * SIDE : 4 * SIDE], refs[4 * SIDE]
    inputs, turned, weights, values, moved, in_sem, weight_sem = refs[4 * SIDE + 1 :]
    x = place[0]
    rows = blocks[0].shape[0]
    width = turned.shape[1]
    units = out.shape[1]
    in_copies = [
        pltpu.make_async_copy(b, inputs.at[pl.ds(i * rows, rows)], in_sem.at[i])
        for i, b in enumerate(blocks)
    ]
    weight_copies = [
        pltpu.make_async_copy(v, weights.at[i], weight_sem.at[i]) for i, v in enumerate(sides)
    ]
    for c in in_copies + weight_copies:
        c.start()
    for p in range(SIDE):
        in_copies[2 * p].wait()
        in_copies[2 * p + 1].wait()
        at = slice(2 * p * rows, 2 * (p + 1) * rows)
        for t in range(SIDE):
            turned[t, :, at] = jnp.transpose(inputs[at, t * width : (t + 1) * width])
    sums = [0.0, 0.0]
    for s in range(SIDE):
        these = turned[(x + SIDE - s) % SIDE]
        for k in range(2):
            weight_copies[2 * s + k].wait()
            sums[k] = sums[k] + jnp.dot(
                weights[2 * s + k], these, preferred_element_type=jnp.float32
            )
    value = jax.nn.silu(sums[0]) * sums[1]
    spare = values.shape[1] - units
    value = jnp.concatenate([value, jnp.zeros((spare, value.shape[1]), jnp.float32)], axis=0)
    values[...] = jnp.transpose(value)
    slots = source.shape[0]
    block = values.shape[0] // slots
    for d in range(slots):
        moved[d : d + 1] = values[pl.ds(source[d] * block + block - 1, 1)]
    for d in range(slots):
        values[(d + 1) * block - 1 : (d + 1) * block] = moved[d : d + 1]
    out[...] = values[:, :units].astype(jnp.bfloat16)


def gate_up_act(place, source, blocks, sides):
    rows, features = blocks[0].shape
    rows = rows * len(blocks)
    units, width = sides[0].shape
    padded = -(-units // HD) * HD
    return pl.pallas_call(
        gate_up_kernel,
        out_shape=jax.ShapeDtypeStruct((rows, units), jnp.bfloat16),
        in_specs=[SM, SM] + [HBM] * (4 * SIDE),
        out_specs=VM,
        scratch_shapes=[
            pltpu.VMEM((rows, features), jnp.bfloat16),
            pltpu.VMEM((SIDE, width, rows), jnp.bfloat16),
            pltpu.VMEM((2 * SIDE, units, width), jnp.bfloat16),
            pltpu.VMEM((rows, padded), jnp.float32),
            pltpu.VMEM((source.shape[0], padded), jnp.float32),
            pltpu.SemaphoreType.DMA((2 * SIDE,)),
            pltpu.SemaphoreType.DMA((2 * SIDE,)),
        ],
        compiler_params=params(26),
        name="gate_up_act",
    )(place, source, *map(in_hbm, blocks), *map(in_hbm, sides))


def down_kernel(base, place, slot, weight, *refs):
    acts, homes, outs = refs[:SIDE], refs[SIDE : 2 * SIDE], refs[2 * SIDE : 3 * SIDE]
    inputs, sem = refs[3 * SIDE :]
    x = place[0]
    rows = inputs.shape[1]
    block = homes[0].shape[0]

    def copy(s):
        return pltpu.make_async_copy(acts[s].at[pl.ds(base * block, rows)], inputs.at[s], sem.at[s])

    order = (0, 1, 3, 2)
    for s in order:
        copy(s).start()
    line = lax.broadcasted_iota(jnp.int32, homes[0].shape, 0)
    for s in order:
        from_x = (x + SIDE - s) % SIDE
        copy(s).wait()
        values = jnp.dot(inputs[s], weight[...], preferred_element_type=jnp.float32)
        home = homes[s][...].astype(jnp.float32)
        moves = (line == block - 1) & (from_x == SIDE - 1)
        for d in range(rows // block):
            value = values[d * block : (d + 1) * block]
            adds = moves & (slot[0] == base + d)
            if base + d == 0:
                adds = adds | jnp.logical_not(moves)
            value = value + jnp.where(adds, home, 0.0)
            outs[d // SIDE][d % SIDE, from_x] = value.astype(jnp.bfloat16)


def down(base, place, slot, weight, acts, homes):
    block, width = homes[0].shape
    rows = acts[0].shape[0] // 2
    out = jax.ShapeDtypeStruct((SIDE, SIDE, block, width), jnp.bfloat16)
    return pl.pallas_call(
        lambda *refs: down_kernel(base, *refs),
        out_shape=[out] * SIDE,
        in_specs=[SM, SM, VM] + [HBM] * SIDE + [VM] * SIDE,
        out_specs=[VM] * SIDE,
        scratch_shapes=[
            pltpu.VMEM((SIDE, rows, weight.shape[0]), jnp.bfloat16),
            pltpu.SemaphoreType.DMA((SIDE,)),
        ],
        compiler_params=params(24),
        name="down",
    )(place, slot, weight, *map(in_hbm, acts), *homes)


def slot_sources(dest):
    z, y, c = (lax.axis_index(a) for a in REP)
    other, second, first = jnp.meshgrid(
        jnp.arange(2), jnp.arange(SIDE), jnp.arange(SIDE), indexing="ij"
    )
    core = (c + other) % 2
    slot_z = (z - jnp.where(core == 0, first, second)) % SIDE
    slot_y = (y - jnp.where(core == 0, second, first)) % SIDE
    group = ((slot_z * SIDE + slot_y) * 2 + core).reshape(-1)
    target = jnp.sum(
        jnp.where(group[:, None] == jnp.arange(dest.shape[0])[None, :], dest[None, :], 0), axis=1
    )
    hit = group[:, None] == target[None, :]
    return jnp.sum(jnp.where(hit, jnp.arange(group.shape[0])[None, :], 0), axis=1)


def add(values):
    return sum(v.astype(jnp.float32) for v in values).astype(jnp.bfloat16)


def local(
    hidden_in,
    query,
    new_kv,
    pool,
    page_table,
    lengths,
    dest,
    out_weight,
    norm_gain,
    gate_up,
    down_weight,
):
    rows_here, width = hidden_in.shape
    x = lax.axis_index("x")
    place = jnp.stack([x, lax.axis_index(REP)]).astype(jnp.int32)

    gate, up = split(jnp.transpose(gate_up, (1, 2, 0)))
    gate_1, up_3 = along_x(gate, 1), along_x(up, 3)

    source = slot_sources(dest).astype(jnp.int32)
    slots = source.shape[0]
    identity = jnp.arange(slots, dtype=jnp.int32)
    slot = jnp.sum(jnp.where(source == 0, identity, 0))[None]
    source = jnp.where(x == SIDE - 1, source, identity)

    parts = attend_project(
        page_table.T, lengths, place, query, new_kv, hidden_in, norm_gain, pool, out_weight
    )
    parts = [parts[0]] + [along_x(parts[s], s) for s in (1, 2, 3)]
    *parts, gate_1, up_3 = lax.optimization_barrier((*parts, gate_1, up_3))
    gate_2, up_2 = along_x(gate_1, 1), along_x(up_3, 3)
    normed, *pieces = normalise(place, parts, width)

    first = join([normed] + [along_chips(normed, s, True) for s in (1, 2, 3)])
    first, gate, up, gate_2, up_2 = lax.optimization_barrier((first, gate, up, gate_2, up_2))
    gate_3, up_1 = along_x(gate, 3), along_x(up, 1)
    sides = (gate, up, gate_1, up_1, gate_2, up_2, gate_3, up_3)
    second = [first] + [along_chips(first, s, False) for s in (1, 2, 3)]
    blocks = second + [other_core(v) for v in second]
    homes = [pieces[0]] + [along_x(pieces[s], s) for s in (1, 2, 3)]
    activated = gate_up_act(place, source, blocks, sides)
    activated, *homes = lax.optimization_barrier((activated, *homes))
    acts = [activated] + [along_x(activated, s) for s in (1, 2, 3)]

    theirs = down(slots // 2, place, slot, down_weight, acts, homes)
    theirs = [other_core(v) for v in theirs]
    mine = down(0, place, slot, down_weight, acts, homes)
    summed = [add(pair) for pair in zip(mine, theirs)]
    total = add([summed[0]] + [along_chips(summed[s], -s, False) for s in (1, 2, 3)])
    out = add([total[0]] + [along_chips(total[s], -s, True) for s in (1, 2, 3)])
    return out.reshape(rows_here, width)


def solution(mesh):
    chips = Mesh(mesh.devices.reshape(SIDE, SIDE, 2, SIDE), ("z", "y", "c", "x"))
    return jax.shard_map(
        local,
        mesh=chips,
        in_specs=(
            P(REP, "x"),
            P(REP, "x"),
            P(REP, None, "x"),
            P(REP, None, None, "x"),
            P(REP, None),
            P(),
            P(),
            P("x", None),
            P("x"),
            P("x", None, REP),
            P(REP, "x"),
        ),
        out_specs=P(REP, "x"),
        check_vma=False,
    )
```

```python
import jax
import jax.numpy as jnp
from jax import lax
from jax.experimental import pallas as pl
from jax.experimental.pallas import tpu as pltpu
from jax.sharding import Mesh, PartitionSpec as P

HD = 128
EPSILON = 1e-05
REP = ("z", "y", "c")
SIDE = 4
GROUP_LANES = 128
HBM = pl.BlockSpec(memory_space=pltpu.HBM)
VM = pl.BlockSpec(memory_space=pltpu.VMEM)
SM = pl.BlockSpec(memory_space=pltpu.SMEM)


def params(megabytes):
    return pltpu.CompilerParams(vmem_limit_bytes=megabytes * 1024 * 1024)


def in_hbm(value):
    return pltpu.with_memory_space_constraint(value, pltpu.HBM)


def cost(flops, moved):
    return pl.CostEstimate(flops=int(flops), transcendentals=0, bytes_accessed=int(moved))


def x_ring(shift):
    return [(i, (i + shift) % SIDE) for i in range(SIDE)]


def chip_ring(shift, first):
    pairs = []
    for z in range(SIDE):
        for y in range(SIDE):
            for c in range(2):
                if (c == 0) == first:
                    to = (((z + shift) % SIDE) * SIDE + y) * 2 + c
                else:
                    to = (z * SIDE + (y + shift) % SIDE) * 2 + c
                pairs.append(((z * SIDE + y) * 2 + c, to))
    return pairs


def along_x(value, shift):
    return lax.ppermute(value, "x", x_ring(shift))


def along_chips(value, shift, first):
    return lax.ppermute(value, REP, chip_ring(shift, first))


def other_core(value):
    return lax.ppermute(value, "c", [(0, 1), (1, 0)])


def attend_kernel(place, tables, spans, query, new_kv, hidden, gain, pool, weight, *refs):
    outs = refs[:SIDE]
    pages, weights, queries, pairs, homes, gains, table, lengths, by_head, heads, rows = refs[
        SIDE : SIDE + 11
    ]
    page_sem, weight_sem, sem = refs[SIDE + 11 :]
    groups, many, span_rows = pages.shape[:3]
    page_rows = pool.shape[1]
    requests, width = hidden.shape
    group = width // HD
    lanes = many * group
    block = requests // SIDE
    scale = HD ** (-0.5)
    x = place[0]
    home = place[1] * requests

    def weight_copy(n):
        return pltpu.make_async_copy(
            weight.at[:, pl.ds(n * width, width)], weights.at[n], weight_sem.at[n]
        )

    small = [
        pltpu.make_async_copy(source, into, sem.at[n])
        for n, (source, into) in enumerate(
            (
                (tables, table),
                (spans, lengths),
                (query, queries),
                (new_kv, pairs),
                (hidden, homes),
                (gain, gains),
            )
        )
    ]
    for copy in small:
        copy.start()
    small[0].wait()
    for g in range(groups):
        for i in range(many):
            for j in range(2):
                pltpu.make_async_copy(
                    pool.at[table[j, g * many + i]],
                    pages.at[g, i, pl.ds(j * page_rows, page_rows)],
                    page_sem.at[g],
                ).start()
    for n in range(SIDE):
        weight_copy(n).start()
    for copy in small[1:]:
        copy.wait()

    row = lax.broadcasted_iota(jnp.int32, (span_rows, lanes), 0)
    is_key = row % 2 == 0
    position = row // 2
    owner = lax.broadcasted_iota(jnp.int32, (HD, lanes), 1) // group
    lane = lax.broadcasted_iota(jnp.int32, (1, lanes), 1) // group

    def one_group(g):
        r0 = g * many
        for h in range(group):
            by_head[g, pl.ds(h, many, stride=group), :] = queries[
                r0 : r0 + many, h * HD : (h + 1) * HD
            ].astype(jnp.float32)
        q_t = jnp.transpose(by_head[g])
        sides = jnp.concatenate(
            [jnp.where(owner == i, q_t, 0.0).astype(jnp.bfloat16) for i in range(many)], axis=0
        )
        span = jnp.zeros((1, lanes), jnp.int32)
        for i in range(many):
            span = jnp.where(lane == i, lengths[home + r0 + i], span)
        pltpu.make_async_copy(pages.at[g], pages.at[g], page_sem.at[g]).wait()
        cached = jnp.concatenate([pages[g, i] for i in range(many)], axis=1)
        scores = jnp.dot(cached, sides, preferred_element_type=jnp.float32) * scale
        fresh = [pairs[r0 + i].astype(jnp.float32) for i in range(many)]
        own = jnp.dot(
            jnp.concatenate(fresh, axis=1).astype(jnp.bfloat16),
            sides,
            preferred_element_type=jnp.float32,
        )[0:1] * scale
        valid = is_key & (position < span)
        peak = jnp.maximum(
            jnp.max(jnp.where(valid, scores, -jnp.inf), axis=0, keepdims=True), own
        )
        w = jnp.where(valid, jnp.exp(scores - peak), 0.0)
        w_own = jnp.exp(own - peak)
        total = jnp.sum(w, axis=0, keepdims=True) + w_own
        line = lax.broadcasted_iota(jnp.int32, (HD, lanes), 0)
        w = jnp.transpose(pltpu.roll(w, 1, 0)).astype(jnp.bfloat16)
        last = jnp.transpose(jnp.where(line == 0, w_own, total))
        w_own = last[:, 0:1].astype(jnp.bfloat16).astype(jnp.float32)
        total = last[:, 1:2]
        for i in range(0, many, 2):
            two = jnp.concatenate([pages[g, i], pages[g, i + 1]], axis=1)
            mixed = jnp.dot(
                w[i * group : (i + 2) * group], two, preferred_element_type=jnp.float32
            )
            for k in range(2):
                at = slice((i + k) * group, (i + k + 1) * group)
                value = mixed[k * group : (k + 1) * group, k * HD : (k + 1) * HD]
                value = (value + w_own[at] * fresh[i + k][1:2]) / total[at]
                heads[pl.ds((r0 + i + k) * group, group), :] = value

    for g in range(groups):
        one_group(g)
    attention = jnp.concatenate(
        [heads[pl.ds(h, requests, stride=group), :].astype(jnp.bfloat16) for h in range(group)],
        axis=1,
    )
    for n in range(SIDE):
        weight_copy(n).wait()
        part = jnp.dot(attention, weights[n], preferred_element_type=jnp.float32)
        part = part + jnp.where(x == n, homes[...].astype(jnp.float32), 0.0)
        part = part.astype(jnp.bfloat16)
        for t in range(SIDE):
            rows[t, :, n * width : (n + 1) * width] = part[t * block : (t + 1) * block]
    high = gains[...].astype(jnp.bfloat16).astype(jnp.float32)
    extra = jnp.concatenate([high, gains[...] - high], axis=0).astype(jnp.bfloat16)
    for s in range(SIDE):
        outs[s][:, : SIDE * width] = rows[(x + s) % SIDE]
        outs[s][:, SIDE * width :] = extra


def attend_project(table, lengths, place, query, new_kv, hidden, gain, pool, weight):
    requests, width = hidden.shape
    block = requests // SIDE
    group = width // HD
    many = GROUP_LANES // group
    groups = requests // many
    page_rows = pool.shape[1] * pool.shape[2]
    out = jax.ShapeDtypeStruct((block, SIDE * width + HD), jnp.bfloat16)
    return pl.pallas_call(
        attend_kernel,
        out_shape=[out] * SIDE,
        in_specs=[SM] + [HBM] * 8,
        out_specs=[VM] * SIDE,
        scratch_shapes=[
            pltpu.VMEM((groups, many, 2 * page_rows, HD), jnp.bfloat16),
            pltpu.VMEM((SIDE, weight.shape[0], width), jnp.bfloat16),
            pltpu.VMEM(query.shape, jnp.bfloat16),
            pltpu.VMEM(new_kv.shape, jnp.bfloat16),
            pltpu.VMEM(hidden.shape, jnp.bfloat16),
            pltpu.VMEM((group, HD), jnp.float32),
            pltpu.SMEM(table.shape, jnp.int32),
            pltpu.SMEM(lengths.shape, jnp.int32),
            pltpu.VMEM((groups, many * group, HD), jnp.float32),
            pltpu.VMEM((requests * group, HD), jnp.float32),
            pltpu.VMEM((SIDE, block, SIDE * width), jnp.bfloat16),
            pltpu.SemaphoreType.DMA((groups,)),
            pltpu.SemaphoreType.DMA((SIDE,)),
            pltpu.SemaphoreType.DMA((6,)),
        ],
        compiler_params=params(36),
        cost_estimate=cost(2 * requests * width * SIDE * width, 2 * (pool.size + weight.size)),
        name="attend_project",
    )(
        place,
        in_hbm(table),
        in_hbm(lengths),
        in_hbm(query),
        in_hbm(new_kv),
        in_hbm(hidden),
        in_hbm(gain.reshape(group, HD)),
        in_hbm(pool.reshape(pool.shape[0], page_rows, HD)),
        in_hbm(weight),
    )


def norm_kernel(place, *refs):
    parts, (normed, kept, gains) = refs[:SIDE], refs[SIDE:]
    x = place[0]
    width = kept.shape[2]
    lines = width // HD
    for s in range(SIDE):
        extra = parts[s][:, SIDE * width :].astype(jnp.float32)
        gains[(x + SIDE - s) % SIDE] = extra[:lines] + extra[lines:]
    square = 0.0
    residual = []
    for n in range(SIDE):
        at = slice(n * width, (n + 1) * width)
        value = sum(p[:, at].astype(jnp.float32) for p in parts)
        square = square + jnp.sum(value * value, axis=1, keepdims=True)
        kept[n] = value.astype(jnp.bfloat16)
        residual.append(value)
    factor = lax.rsqrt(square / (SIDE * width) + EPSILON)
    for n in range(SIDE):
        gain = gains[n]
        for j in range(lines):
            value = residual[n][:, j * HD : (j + 1) * HD] * factor * gain[j : j + 1]
            normed[:, n * width + j * HD : n * width + (j + 1) * HD] = value.astype(jnp.bfloat16)


def normalise(place, parts, width):
    block = parts[0].shape[0]
    return pl.pallas_call(
        norm_kernel,
        out_shape=[
            jax.ShapeDtypeStruct((block, SIDE * width), jnp.bfloat16),
            jax.ShapeDtypeStruct((SIDE, block, width), jnp.bfloat16),
        ],
        in_specs=[SM] + [VM] * SIDE,
        out_specs=[VM, VM],
        scratch_shapes=[pltpu.VMEM((SIDE, width // HD, HD), jnp.float32)],
        compiler_params=params(16),
        cost_estimate=cost(0, 12 * SIDE * block * width),
        name="normalise",
    )(place, *parts)


def join_kernel(*refs):
    parts, out = refs[:-1], refs[-1]
    rows = parts[0].shape[0]
    for i, part in enumerate(parts):
        out[i * rows : (i + 1) * rows] = part[...]


def join(parts):
    rows, width = parts[0].shape
    return pl.pallas_call(
        join_kernel,
        out_shape=jax.ShapeDtypeStruct((len(parts) * rows, width), parts[0].dtype),
        in_specs=[VM] * len(parts),
        out_specs=VM,
        compiler_params=params(4),
        cost_estimate=cost(0, 4 * len(parts) * rows * width),
        name="join",
    )(*parts)


def split_kernel(both, gate, up, sem):
    copies = [
        pltpu.make_async_copy(both.at[k], into, sem.at[k]) for k, into in enumerate((gate, up))
    ]
    for c in copies:
        c.start()
    for c in copies:
        c.wait()


def split(both):
    half = jax.ShapeDtypeStruct(both.shape[1:], both.dtype)
    return pl.pallas_call(
        split_kernel,
        out_shape=[half, half],
        in_specs=[HBM],
        out_specs=[VM, VM],
        scratch_shapes=[pltpu.SemaphoreType.DMA((2,))],
        compiler_params=params(4),
        name="split",
    )(in_hbm(both))


def gate_up_kernel(place, source, *refs):
    blocks, sides, outs = refs[: 2 * SIDE], refs[2 * SIDE : 4 * SIDE], refs[4 * SIDE : 4 * SIDE + 2]
    turned, weights, values, moved, sem = refs[4 * SIDE + 2 :]
    x = place[0]
    rows = blocks[0].shape[0]
    units, width = sides[0].shape
    apart = weights.shape[0] // 2
    copies = []
    for i, side in enumerate(sides):
        start = pl.multiple_of(((x + SIDE - i // 2) % SIDE) * width, width)
        into = weights.at[pl.ds((i % 2) * apart, units), pl.ds(start, width)]
        copies.append(pltpu.make_async_copy(side, into, sem.at[i]))
    for c in copies:
        c.start()
    for p in range(SIDE):
        pair = jnp.concatenate([blocks[2 * p][...], blocks[2 * p + 1][...]], axis=0)
        turned[:, 2 * p * rows : 2 * (p + 1) * rows] = jnp.transpose(pair)
    for c in copies:
        c.wait()
    both = jnp.dot(weights[...], turned[...], preferred_element_type=jnp.float32)
    value = jax.nn.silu(both[:units]) * both[apart : apart + units]
    spare = values.shape[1] - units
    value = jnp.concatenate([value, jnp.zeros((spare, value.shape[1]), jnp.float32)], axis=0)
    values[...] = jnp.transpose(value)
    slots = source.shape[0]
    block = values.shape[0] // slots
    for d in range(slots):
        moved[d : d + 1] = values[pl.ds(source[d] * block + block - 1, 1)]
    for d in range(slots):
        values[(d + 1) * block - 1 : (d + 1) * block] = moved[d : d + 1]
    half = values.shape[0] // 2
    for k in range(2):
        outs[k][...] = values[k * half : (k + 1) * half, :units].astype(jnp.bfloat16)


def gate_up_act(place, source, blocks, sides):
    rows, features = blocks[0].shape
    rows = rows * len(blocks)
    units = sides[0].shape[0]
    padded = -(-units // HD) * HD
    return pl.pallas_call(
        gate_up_kernel,
        out_shape=[jax.ShapeDtypeStruct((rows // 2, units), jnp.bfloat16)] * 2,
        in_specs=[SM, SM] + [VM] * (2 * SIDE) + [HBM] * (2 * SIDE),
        out_specs=[VM, VM],
        scratch_shapes=[
            pltpu.VMEM((features, rows), jnp.bfloat16),
            pltpu.VMEM((2 * (-(-units // 16) * 16), features), jnp.bfloat16),
            pltpu.VMEM((rows, padded), jnp.float32),
            pltpu.VMEM((source.shape[0], padded), jnp.float32),
            pltpu.SemaphoreType.DMA((2 * SIDE,)),
        ],
        compiler_params=params(24),
        cost_estimate=cost(4 * rows * features * units, 10 * units * features),
        name="gate_up_act",
    )(place, source, *blocks, *map(in_hbm, sides))


def down_kernel(base, start, place, slot, weight, *refs):
    acts, homes, theirs, out = refs[:SIDE], refs[SIDE], refs[SIDE + 1 : -1], refs[-1]
    x = place[0]
    block = homes.shape[1]
    rows = SIDE * block
    inputs = jnp.concatenate([a[start * block : start * block + rows] for a in acts], axis=0)
    values = jnp.dot(inputs, weight[...], preferred_element_type=jnp.float32)
    line = lax.broadcasted_iota(jnp.int32, homes.shape[1:], 0)
    for s in range(SIDE):
        from_x = (x + SIDE - s) % SIDE
        home = homes[from_x].astype(jnp.float32)
        moves = (line == block - 1) & (from_x == SIDE - 1)
        for d in range(SIDE):
            value = values[s * rows + d * block : s * rows + (d + 1) * block]
            adds = moves & (slot[0] == base + d)
            if base + d == 0:
                adds = adds | jnp.logical_not(moves)
            value = value + jnp.where(adds, home, 0.0)
            for other in theirs:
                value = value + other[d, from_x].astype(jnp.float32)
            out[d, from_x] = value.astype(jnp.bfloat16)


def down(base, start, place, slot, weight, acts, homes, theirs=()):
    block, width = homes.shape[1:]
    return pl.pallas_call(
        lambda *refs: down_kernel(base, start, *refs),
        out_shape=jax.ShapeDtypeStruct((SIDE, SIDE, block, width), jnp.bfloat16),
        in_specs=[SM, SM, VM] + [VM] * (SIDE + 1 + len(theirs)),
        out_specs=VM,
        compiler_params=params(12),
        cost_estimate=cost(2 * SIDE * SIDE * block * weight.size, 2 * weight.size),
        name="down",
    )(place, slot, weight, *acts, homes, *theirs)


def slot_sources(dest):
    z, y, c = (lax.axis_index(a) for a in REP)
    other, second, first = jnp.meshgrid(
        jnp.arange(2), jnp.arange(SIDE), jnp.arange(SIDE), indexing="ij"
    )
    core = (c + other) % 2
    slot_z = (z - jnp.where(core == 0, first, second)) % SIDE
    slot_y = (y - jnp.where(core == 0, second, first)) % SIDE
    group = ((slot_z * SIDE + slot_y) * 2 + core).reshape(-1)
    target = jnp.sum(
        jnp.where(group[:, None] == jnp.arange(dest.shape[0])[None, :], dest[None, :], 0), axis=1
    )
    hit = group[:, None] == target[None, :]
    return jnp.sum(jnp.where(hit, jnp.arange(group.shape[0])[None, :], 0), axis=1)


def add(values):
    return sum(v.astype(jnp.float32) for v in values).astype(jnp.bfloat16)


def local(
    hidden_in,
    query,
    new_kv,
    pool,
    page_table,
    lengths,
    dest,
    out_weight,
    norm_gain,
    gate_up,
    down_weight,
):
    rows_here, width = hidden_in.shape
    x = lax.axis_index("x")
    place = jnp.stack([x, lax.axis_index(REP)]).astype(jnp.int32)

    gate, up = split(jnp.transpose(gate_up, (1, 2, 0)))
    gate_1, up_3 = along_x(gate, 1), along_x(up, 3)

    source = slot_sources(dest).astype(jnp.int32)
    slots = source.shape[0]
    identity = jnp.arange(slots, dtype=jnp.int32)
    slot = jnp.sum(jnp.where(source == 0, identity, 0))[None]
    source = jnp.where(x == SIDE - 1, source, identity)

    parts = attend_project(
        page_table.T, lengths, place, query, new_kv, hidden_in, norm_gain, pool, out_weight
    )
    parts = [parts[0]] + [along_x(parts[s], s) for s in (1, 2, 3)]
    normed, kept = normalise(place, parts, width)
    homes = lax.all_to_all(kept, "x", 0, 0, tiled=True)
    normed, gate_1, up_3 = lax.optimization_barrier((normed, gate_1, up_3))
    gate_2, up_2 = along_x(gate_1, 1), along_x(up_3, 3)

    first = join([normed] + [along_chips(normed, s, True) for s in (1, 2, 3)])
    first, gate, up, gate_2, up_2, homes = lax.optimization_barrier(
        (first, gate, up, gate_2, up_2, homes)
    )
    gate_3, up_1 = along_x(gate, 3), along_x(up, 1)
    sides = (gate, up, gate_1, up_1, gate_2, up_2, gate_3, up_3)
    second = [first] + [along_chips(first, s, False) for s in (1, 2, 3)]
    second[0], second[1] = lax.optimization_barrier((second[0], second[1]))
    blocks = second + [other_core(v) for v in second]
    mine, theirs = gate_up_act(place, source, blocks, sides)
    mine, theirs, homes = lax.optimization_barrier((mine, theirs, homes))
    theirs_1, theirs_3 = along_x(theirs, 1), along_x(theirs, 3)
    mine_1, mine_3 = along_x(mine, 1), along_x(mine, 3)
    theirs_2 = along_x(theirs_1, 1)
    theirs_2, theirs_3, mine_1, mine_3 = lax.optimization_barrier(
        (theirs_2, theirs_3, mine_1, mine_3)
    )
    theirs = [theirs, theirs_1, theirs_2, theirs_3]
    mine = [mine, mine_1, along_x(mine_3, 3), mine_3]

    half = slots // 2
    shifts = (2, 1, 3, 0)
    sent = [
        down(half + s * SIDE, s * SIDE, place, slot, down_weight, theirs, homes) for s in shifts
    ]
    sent[1], mine[2] = lax.optimization_barrier((sent[1], mine[2]))
    sent = [other_core(v) for v in sent]
    total = []
    for s, received in zip(shifts, sent):
        value = down(s * SIDE, s * SIDE, place, slot, down_weight, mine, homes, (received,))
        total.append(along_chips(value, -s, False) if s else value)
    total = add(total)
    out = add([total[0]] + [along_chips(total[s], -s, True) for s in (1, 2, 3)])
    return out.reshape(rows_here, width)


def solution(mesh):
    chips = Mesh(mesh.devices.reshape(SIDE, SIDE, 2, SIDE), ("z", "y", "c", "x"))
    return jax.shard_map(
        local,
        mesh=chips,
        in_specs=(
            P(REP, "x"),
            P(REP, "x"),
            P(REP, None, "x"),
            P(REP, None, None, "x"),
            P(REP, None),
            P(),
            P(),
            P("x", None),
            P("x"),
            P("x", None, REP),
            P(REP, "x"),
        ),
        out_specs=P(REP, "x"),
        check_vma=False,
    )
```

```python
import jax
import jax.numpy as jnp
from jax import lax
from jax.experimental import pallas as pl
from jax.experimental.pallas import tpu as pltpu
from jax.sharding import Mesh, PartitionSpec as P

HD = 128
EPSILON = 1e-05
REP = ("z", "y", "c")
SIDE = 4
GROUP_LANES = 128
HBM = pl.BlockSpec(memory_space=pltpu.HBM)
VM = pl.BlockSpec(memory_space=pltpu.VMEM)
SM = pl.BlockSpec(memory_space=pltpu.SMEM)


def params(megabytes):
    return pltpu.CompilerParams(vmem_limit_bytes=megabytes * 1024 * 1024)


def in_hbm(value):
    return pltpu.with_memory_space_constraint(value, pltpu.HBM)


def cost(flops, moved):
    return pl.CostEstimate(flops=int(flops), transcendentals=0, bytes_accessed=int(moved))


def x_ring(shift):
    return [(i, (i + shift) % SIDE) for i in range(SIDE)]


def chip_ring(shift, first):
    pairs = []
    for z in range(SIDE):
        for y in range(SIDE):
            for c in range(2):
                if (c == 0) == first:
                    to = (((z + shift) % SIDE) * SIDE + y) * 2 + c
                else:
                    to = (z * SIDE + (y + shift) % SIDE) * 2 + c
                pairs.append(((z * SIDE + y) * 2 + c, to))
    return pairs


def along_x(value, shift):
    return lax.ppermute(value, "x", x_ring(shift))


def along_chips(value, shift, first):
    return lax.ppermute(value, REP, chip_ring(shift, first))


def other_core(value):
    return lax.ppermute(value, "c", [(0, 1), (1, 0)])


def attend_kernel(place, tables, spans, query, new_kv, hidden, gain, pool, weight, *refs):
    outs = refs[:SIDE]
    pages, weights, queries, pairs, homes, gains, table, lengths, by_head, heads, rows = refs[
        SIDE : SIDE + 11
    ]
    page_sem, weight_sem, sem = refs[SIDE + 11 :]
    groups, many, span_rows = pages.shape[:3]
    page_rows = pool.shape[1]
    requests, width = hidden.shape
    group = width // HD
    lanes = many * group
    block = requests // SIDE
    scale = HD ** (-0.5)
    x = place[0]
    home = place[1] * requests

    def weight_copy(n):
        return pltpu.make_async_copy(
            weight.at[:, pl.ds(n * width, width)], weights.at[n], weight_sem.at[n]
        )

    small = [
        pltpu.make_async_copy(source, into, sem.at[n])
        for n, (source, into) in enumerate(
            (
                (tables, table),
                (spans, lengths),
                (query, queries),
                (new_kv, pairs),
                (hidden, homes),
                (gain, gains),
            )
        )
    ]
    for copy in small:
        copy.start()
    small[0].wait()
    for g in range(groups):
        for i in range(many):
            for j in range(2):
                pltpu.make_async_copy(
                    pool.at[table[j, g * many + i]],
                    pages.at[g, i, pl.ds(j * page_rows, page_rows)],
                    page_sem.at[g],
                ).start()
    for n in range(SIDE):
        weight_copy(n).start()
    for copy in small[1:]:
        copy.wait()

    row = lax.broadcasted_iota(jnp.int32, (span_rows, lanes), 0)
    is_key = row % 2 == 0
    position = row // 2
    owner = lax.broadcasted_iota(jnp.int32, (HD, lanes), 1) // group
    lane = lax.broadcasted_iota(jnp.int32, (1, lanes), 1) // group

    def one_group(g):
        r0 = g * many
        for h in range(group):
            by_head[g, pl.ds(h, many, stride=group), :] = queries[
                r0 : r0 + many, h * HD : (h + 1) * HD
            ].astype(jnp.float32)
        q_t = jnp.transpose(by_head[g])
        sides = jnp.concatenate(
            [jnp.where(owner == i, q_t, 0.0).astype(jnp.bfloat16) for i in range(many)], axis=0
        )
        span = jnp.zeros((1, lanes), jnp.int32)
        for i in range(many):
            span = jnp.where(lane == i, lengths[home + r0 + i], span)
        pltpu.make_async_copy(pages.at[g], pages.at[g], page_sem.at[g]).wait()
        cached = jnp.concatenate([pages[g, i] for i in range(many)], axis=1)
        scores = jnp.dot(cached, sides, preferred_element_type=jnp.float32) * scale
        fresh = [pairs[r0 + i].astype(jnp.float32) for i in range(many)]
        own = jnp.dot(
            jnp.concatenate(fresh, axis=1).astype(jnp.bfloat16),
            sides,
            preferred_element_type=jnp.float32,
        )[0:1] * scale
        valid = is_key & (position < span)
        peak = jnp.maximum(
            jnp.max(jnp.where(valid, scores, -jnp.inf), axis=0, keepdims=True), own
        )
        w = jnp.where(valid, jnp.exp(scores - peak), 0.0)
        w_own = jnp.exp(own - peak)
        total = jnp.sum(w, axis=0, keepdims=True) + w_own
        line = lax.broadcasted_iota(jnp.int32, (HD, lanes), 0)
        w = jnp.transpose(pltpu.roll(w, 1, 0)).astype(jnp.bfloat16)
        last = jnp.transpose(jnp.where(line == 0, w_own, total))
        w_own = last[:, 0:1].astype(jnp.bfloat16).astype(jnp.float32)
        total = last[:, 1:2]
        for i in range(0, many, 2):
            two = jnp.concatenate([pages[g, i], pages[g, i + 1]], axis=1)
            mixed = jnp.dot(
                w[i * group : (i + 2) * group], two, preferred_element_type=jnp.float32
            )
            for k in range(2):
                at = slice((i + k) * group, (i + k + 1) * group)
                value = mixed[k * group : (k + 1) * group, k * HD : (k + 1) * HD]
                value = (value + w_own[at] * fresh[i + k][1:2]) / total[at]
                heads[pl.ds((r0 + i + k) * group, group), :] = value

    for g in range(groups):
        one_group(g)
    attention = jnp.concatenate(
        [heads[pl.ds(h, requests, stride=group), :].astype(jnp.bfloat16) for h in range(group)],
        axis=1,
    )
    for n in range(SIDE):
        weight_copy(n).wait()
        part = jnp.dot(attention, weights[n], preferred_element_type=jnp.float32)
        part = part + jnp.where(x == n, homes[...].astype(jnp.float32), 0.0)
        part = part.astype(jnp.bfloat16)
        for t in range(SIDE):
            rows[t, :, n * width : (n + 1) * width] = part[t * block : (t + 1) * block]
    high = gains[...].astype(jnp.bfloat16).astype(jnp.float32)
    extra = jnp.concatenate([high, gains[...] - high], axis=0).astype(jnp.bfloat16)
    for s in range(SIDE):
        outs[s][:, : SIDE * width] = rows[(x + s) % SIDE]
        outs[s][:, SIDE * width :] = extra


def attend_project(table, lengths, place, query, new_kv, hidden, gain, pool, weight):
    requests, width = hidden.shape
    block = requests // SIDE
    group = width // HD
    many = GROUP_LANES // group
    groups = requests // many
    page_rows = pool.shape[1] * pool.shape[2]
    out = jax.ShapeDtypeStruct((block, SIDE * width + HD), jnp.bfloat16)
    return pl.pallas_call(
        attend_kernel,
        out_shape=[out] * SIDE,
        in_specs=[SM] + [HBM] * 8,
        out_specs=[VM] * SIDE,
        scratch_shapes=[
            pltpu.VMEM((groups, many, 2 * page_rows, HD), jnp.bfloat16),
            pltpu.VMEM((SIDE, weight.shape[0], width), jnp.bfloat16),
            pltpu.VMEM(query.shape, jnp.bfloat16),
            pltpu.VMEM(new_kv.shape, jnp.bfloat16),
            pltpu.VMEM(hidden.shape, jnp.bfloat16),
            pltpu.VMEM((group, HD), jnp.float32),
            pltpu.SMEM(table.shape, jnp.int32),
            pltpu.SMEM(lengths.shape, jnp.int32),
            pltpu.VMEM((groups, many * group, HD), jnp.float32),
            pltpu.VMEM((requests * group, HD), jnp.float32),
            pltpu.VMEM((SIDE, block, SIDE * width), jnp.bfloat16),
            pltpu.SemaphoreType.DMA((groups,)),
            pltpu.SemaphoreType.DMA((SIDE,)),
            pltpu.SemaphoreType.DMA((6,)),
        ],
        compiler_params=params(36),
        cost_estimate=cost(2 * requests * width * SIDE * width, 2 * (pool.size + weight.size)),
        name="attend_project",
    )(
        place,
        in_hbm(table),
        in_hbm(lengths),
        in_hbm(query),
        in_hbm(new_kv),
        in_hbm(hidden),
        in_hbm(gain.reshape(group, HD)),
        in_hbm(pool.reshape(pool.shape[0], page_rows, HD)),
        in_hbm(weight),
    )


def norm_kernel(place, *refs):
    parts, (normed, kept, gains) = refs[:SIDE], refs[SIDE:]
    x = place[0]
    width = kept.shape[2]
    lines = width // HD
    for s in range(SIDE):
        extra = parts[s][:, SIDE * width :].astype(jnp.float32)
        gains[(x + SIDE - s) % SIDE] = extra[:lines] + extra[lines:]
    square = 0.0
    residual = []
    for n in range(SIDE):
        at = slice(n * width, (n + 1) * width)
        value = sum(p[:, at].astype(jnp.float32) for p in parts)
        square = square + jnp.sum(value * value, axis=1, keepdims=True)
        kept[n] = value.astype(jnp.bfloat16)
        residual.append(value)
    factor = lax.rsqrt(square / (SIDE * width) + EPSILON)
    for n in range(SIDE):
        gain = gains[n]
        for j in range(lines):
            value = residual[n][:, j * HD : (j + 1) * HD] * factor * gain[j : j + 1]
            normed[:, n * width + j * HD : n * width + (j + 1) * HD] = value.astype(jnp.bfloat16)


def normalise(place, parts, width):
    block = parts[0].shape[0]
    return pl.pallas_call(
        norm_kernel,
        out_shape=[
            jax.ShapeDtypeStruct((block, SIDE * width), jnp.bfloat16),
            jax.ShapeDtypeStruct((SIDE, block, width), jnp.bfloat16),
        ],
        in_specs=[SM] + [VM] * SIDE,
        out_specs=[VM, VM],
        scratch_shapes=[pltpu.VMEM((SIDE, width // HD, HD), jnp.float32)],
        compiler_params=params(16),
        cost_estimate=cost(0, 12 * SIDE * block * width),
        name="normalise",
    )(place, *parts)


def join_kernel(*refs):
    parts, out = refs[:-1], refs[-1]
    rows = parts[0].shape[0]
    for i, part in enumerate(parts):
        out[i * rows : (i + 1) * rows] = part[...]


def join(parts):
    rows, width = parts[0].shape
    return pl.pallas_call(
        join_kernel,
        out_shape=jax.ShapeDtypeStruct((len(parts) * rows, width), parts[0].dtype),
        in_specs=[VM] * len(parts),
        out_specs=VM,
        compiler_params=params(4),
        cost_estimate=cost(0, 4 * len(parts) * rows * width),
        name="join",
    )(*parts)


def split_kernel(both, gate, up, sem):
    copies = [
        pltpu.make_async_copy(both.at[k], into, sem.at[k]) for k, into in enumerate((gate, up))
    ]
    for c in copies:
        c.start()
    for c in copies:
        c.wait()


def split(both):
    half = jax.ShapeDtypeStruct(both.shape[1:], both.dtype)
    return pl.pallas_call(
        split_kernel,
        out_shape=[half, half],
        in_specs=[HBM],
        out_specs=[VM, VM],
        scratch_shapes=[pltpu.SemaphoreType.DMA((2,))],
        compiler_params=params(4),
        name="split",
    )(in_hbm(both))


def gate_up_kernel(place, source, *refs):
    blocks, sides, outs = refs[: 2 * SIDE], refs[2 * SIDE : 4 * SIDE], refs[4 * SIDE : 4 * SIDE + 2]
    turned, weights, values, moved, sem = refs[4 * SIDE + 2 :]
    x = place[0]
    rows = blocks[0].shape[0]
    units, width = sides[0].shape
    apart = weights.shape[0] // 2
    copies = []
    for i, side in enumerate(sides):
        start = pl.multiple_of(((x + SIDE - i // 2) % SIDE) * width, width)
        into = weights.at[pl.ds((i % 2) * apart, units), pl.ds(start, width)]
        copies.append(pltpu.make_async_copy(side, into, sem.at[i]))
    for c in copies:
        c.start()
    for p in range(SIDE):
        pair = jnp.concatenate([blocks[2 * p][...], blocks[2 * p + 1][...]], axis=0)
        turned[:, 2 * p * rows : 2 * (p + 1) * rows] = jnp.transpose(pair)
    for c in copies:
        c.wait()
    both = jnp.dot(weights[...], turned[...], preferred_element_type=jnp.float32)
    value = jax.nn.silu(both[:units]) * both[apart : apart + units]
    spare = values.shape[1] - units
    value = jnp.concatenate([value, jnp.zeros((spare, value.shape[1]), jnp.float32)], axis=0)
    values[...] = jnp.transpose(value)
    slots = source.shape[0]
    block = values.shape[0] // slots
    for d in range(slots):
        moved[d : d + 1] = values[pl.ds(source[d] * block + block - 1, 1)]
    for d in range(slots):
        values[(d + 1) * block - 1 : (d + 1) * block] = moved[d : d + 1]
    half = values.shape[0] // 2
    for k in range(2):
        outs[k][...] = values[k * half : (k + 1) * half, :units].astype(jnp.bfloat16)


def gate_up_act(place, source, blocks, sides):
    rows, features = blocks[0].shape
    rows = rows * len(blocks)
    units = sides[0].shape[0]
    padded = -(-units // HD) * HD
    return pl.pallas_call(
        gate_up_kernel,
        out_shape=[jax.ShapeDtypeStruct((rows // 2, units), jnp.bfloat16)] * 2,
        in_specs=[SM, SM] + [VM] * (2 * SIDE) + [HBM] * (2 * SIDE),
        out_specs=[VM, VM],
        scratch_shapes=[
            pltpu.VMEM((features, rows), jnp.bfloat16),
            pltpu.VMEM((2 * (-(-units // 16) * 16), features), jnp.bfloat16),
            pltpu.VMEM((rows, padded), jnp.float32),
            pltpu.VMEM((source.shape[0], padded), jnp.float32),
            pltpu.SemaphoreType.DMA((2 * SIDE,)),
        ],
        compiler_params=params(24),
        cost_estimate=cost(4 * rows * features * units, 10 * units * features),
        name="gate_up_act",
    )(place, source, *blocks, *map(in_hbm, sides))


def down_kernel(base, picks, place, slot, weight, *refs):
    acts, homes, refs = refs[:SIDE], refs[SIDE], refs[SIDE + 1 :]
    theirs, outs = refs[: -len(picks)], refs[-len(picks) :]
    x = place[0]
    block = homes.shape[1]
    rows = SIDE * block
    inputs = [a[p * rows : (p + 1) * rows] for p in picks for a in acts]
    values = jnp.dot(
        jnp.concatenate(inputs, axis=0), weight[...], preferred_element_type=jnp.float32
    )
    line = lax.broadcasted_iota(jnp.int32, homes.shape[1:], 0)
    for s in range(SIDE):
        from_x = (x + SIDE - s) % SIDE
        home = homes[from_x].astype(jnp.float32)
        moves = (line == block - 1) & (from_x == SIDE - 1)
        for n, p in enumerate(picks):
            for d in range(SIDE):
                at = (n * SIDE + s) * rows + d * block
                value = values[at : at + block]
                here = base + p * SIDE + d
                adds = moves & (slot[0] == here)
                if here == 0:
                    adds = adds | jnp.logical_not(moves)
                value = value + jnp.where(adds, home, 0.0)
                for other in theirs:
                    value = value + other[d, from_x].astype(jnp.float32)
                outs[n][d, from_x] = value.astype(jnp.bfloat16)


def down(base, picks, place, slot, weight, acts, homes, theirs=()):
    block, width = homes.shape[1:]
    out = jax.ShapeDtypeStruct((SIDE, SIDE, block, width), jnp.bfloat16)
    return pl.pallas_call(
        lambda *refs: down_kernel(base, picks, *refs),
        out_shape=[out] * len(picks),
        in_specs=[SM, SM, VM] + [VM] * (SIDE + 1 + len(theirs)),
        out_specs=[VM] * len(picks),
        compiler_params=params(16),
        cost_estimate=cost(
            2 * len(picks) * SIDE * SIDE * block * weight.size, 2 * len(picks) * weight.size
        ),
        name="down",
    )(place, slot, weight, *acts, homes, *theirs)


def slot_sources(dest):
    z, y, c = (lax.axis_index(a) for a in REP)
    other, second, first = jnp.meshgrid(
        jnp.arange(2), jnp.arange(SIDE), jnp.arange(SIDE), indexing="ij"
    )
    core = (c + other) % 2
    slot_z = (z - jnp.where(core == 0, first, second)) % SIDE
    slot_y = (y - jnp.where(core == 0, second, first)) % SIDE
    group = ((slot_z * SIDE + slot_y) * 2 + core).reshape(-1)
    target = jnp.sum(
        jnp.where(group[:, None] == jnp.arange(dest.shape[0])[None, :], dest[None, :], 0), axis=1
    )
    hit = group[:, None] == target[None, :]
    return jnp.sum(jnp.where(hit, jnp.arange(group.shape[0])[None, :], 0), axis=1)


def add(values):
    return sum(v.astype(jnp.float32) for v in values).astype(jnp.bfloat16)


def local(
    hidden_in,
    query,
    new_kv,
    pool,
    page_table,
    lengths,
    dest,
    out_weight,
    norm_gain,
    gate_up,
    down_weight,
):
    rows_here, width = hidden_in.shape
    x = lax.axis_index("x")
    place = jnp.stack([x, lax.axis_index(REP)]).astype(jnp.int32)

    gate, up = split(jnp.transpose(gate_up, (1, 2, 0)))
    gate_1, up_3 = along_x(gate, 1), along_x(up, 3)

    source = slot_sources(dest).astype(jnp.int32)
    slots = source.shape[0]
    identity = jnp.arange(slots, dtype=jnp.int32)
    slot = jnp.sum(jnp.where(source == 0, identity, 0))[None]
    source = jnp.where(x == SIDE - 1, source, identity)

    parts = attend_project(
        page_table.T, lengths, place, query, new_kv, hidden_in, norm_gain, pool, out_weight
    )
    parts = [parts[0]] + [along_x(parts[s], s) for s in (1, 2, 3)]
    normed, kept = normalise(place, parts, width)
    homes = lax.all_to_all(kept, "x", 0, 0, tiled=True)
    normed, gate_1, up_3 = lax.optimization_barrier((normed, gate_1, up_3))
    gate_2, up_2 = along_x(gate_1, 1), along_x(up_3, 3)

    first = join([normed] + [along_chips(normed, s, True) for s in (1, 2, 3)])
    first, gate, up, gate_2, up_2, homes = lax.optimization_barrier(
        (first, gate, up, gate_2, up_2, homes)
    )
    gate_3, up_1 = along_x(gate, 3), along_x(up, 1)
    sides = (gate, up, gate_1, up_1, gate_2, up_2, gate_3, up_3)
    second = [first] + [along_chips(first, s, False) for s in (1, 2, 3)]
    second[0], second[1] = lax.optimization_barrier((second[0], second[1]))
    blocks = second + [other_core(v) for v in second]
    mine, theirs = gate_up_act(place, source, blocks, sides)
    mine, theirs, homes = lax.optimization_barrier((mine, theirs, homes))
    theirs_1, theirs_3 = along_x(theirs, 1), along_x(theirs, 3)
    mine_1, mine_3 = along_x(mine, 1), along_x(mine, 3)
    theirs_2 = along_x(theirs_1, 1)
    theirs_2, theirs_3, mine_1, mine_3 = lax.optimization_barrier(
        (theirs_2, theirs_3, mine_1, mine_3)
    )
    theirs = [theirs, theirs_1, theirs_2, theirs_3]
    mine = [mine, mine_1, along_x(mine_3, 3), mine_3]

    half = slots // 2
    shifts = (2, 1, 3, 0)
    pairs = ((2, 1), (3, 0))
    sent = [
        list(down(half, picks, place, slot, down_weight, theirs, homes)) for picks in pairs
    ]
    sent[1][0], mine[2] = lax.optimization_barrier((sent[1][0], mine[2]))
    received = [other_core(value) for values in sent for value in values]
    total = []
    for s, value in zip((2, 1, 3, 0), received):
        if total:
            value, _ = lax.optimization_barrier((value, made))
        (made,) = down(0, (s,), place, slot, down_weight, mine, homes, (value,))
        total.append(along_chips(made, -s, False) if s else made)
    total = add(total)
    out = add([along_chips(total[s], -s, True) for s in (2, 1, 3)] + [total[0]])
    return out.reshape(rows_here, width)


def solution(mesh):
    chips = Mesh(mesh.devices.reshape(SIDE, SIDE, 2, SIDE), ("z", "y", "c", "x"))
    return jax.shard_map(
        local,
        mesh=chips,
        in_specs=(
            P(REP, "x"),
            P(REP, "x"),
            P(REP, None, "x"),
            P(REP, None, None, "x"),
            P(REP, None),
            P(),
            P(),
            P("x", None),
            P("x"),
            P("x", None, REP),
            P(REP, "x"),
        ),
        out_specs=P(REP, "x"),
        check_vma=False,
    )
```

```python
import jax
import jax.numpy as jnp
from jax import lax
from jax.experimental import pallas as pl
from jax.experimental.pallas import tpu as pltpu
from jax.sharding import Mesh, PartitionSpec as P

HD = 128
EPSILON = 1e-05
REP = ("z", "y", "c")
SIDE = 4
GROUP_LANES = 128
HBM = pl.BlockSpec(memory_space=pltpu.HBM)
VM = pl.BlockSpec(memory_space=pltpu.VMEM)
SM = pl.BlockSpec(memory_space=pltpu.SMEM)


def params(megabytes):
    return pltpu.CompilerParams(vmem_limit_bytes=megabytes * 1024 * 1024)


def in_hbm(value):
    return pltpu.with_memory_space_constraint(value, pltpu.HBM)


def cost(flops, moved):
    return pl.CostEstimate(flops=int(flops), transcendentals=0, bytes_accessed=int(moved))


def x_ring(shift):
    return [(i, (i + shift) % SIDE) for i in range(SIDE)]


def chip_ring(shift, first):
    pairs = []
    for z in range(SIDE):
        for y in range(SIDE):
            for c in range(2):
                if (c == 0) == first:
                    to = (((z + shift) % SIDE) * SIDE + y) * 2 + c
                else:
                    to = (z * SIDE + (y + shift) % SIDE) * 2 + c
                pairs.append(((z * SIDE + y) * 2 + c, to))
    return pairs


def along_x(value, shift):
    return lax.ppermute(value, "x", x_ring(shift))


def along_chips(value, shift, first):
    return lax.ppermute(value, REP, chip_ring(shift, first))


def other_core(value):
    return lax.ppermute(value, "c", [(0, 1), (1, 0)])


def attend_kernel(place, tables, spans, query, new_kv, hidden, gain, pool, weight, *refs):
    outs = refs[:SIDE]
    pages, weights, queries, pairs, homes, gains, table, lengths, by_head, heads, rows = refs[
        SIDE : SIDE + 11
    ]
    page_sem, weight_sem, sem = refs[SIDE + 11 :]
    groups, many, span_rows = pages.shape[:3]
    page_rows = pool.shape[1]
    requests, width = hidden.shape
    group = width // HD
    lanes = many * group
    block = requests // SIDE
    scale = HD ** (-0.5)
    x = place[0]
    home = place[1] * requests

    def weight_copy(n):
        return pltpu.make_async_copy(
            weight.at[:, pl.ds(n * width, width)], weights.at[n], weight_sem.at[n]
        )

    small = [
        pltpu.make_async_copy(source, into, sem.at[n])
        for n, (source, into) in enumerate(
            (
                (tables, table),
                (spans, lengths),
                (query, queries),
                (new_kv, pairs),
                (hidden, homes),
                (gain, gains),
            )
        )
    ]
    for copy in small:
        copy.start()
    small[0].wait()
    for g in range(groups):
        for i in range(many):
            for j in range(2):
                pltpu.make_async_copy(
                    pool.at[table[j, g * many + i]],
                    pages.at[g, i, pl.ds(j * page_rows, page_rows)],
                    page_sem.at[g],
                ).start()
    for n in range(SIDE):
        weight_copy(n).start()
    for copy in small[1:]:
        copy.wait()

    row = lax.broadcasted_iota(jnp.int32, (span_rows, lanes), 0)
    is_key = row % 2 == 0
    position = row // 2
    owner = lax.broadcasted_iota(jnp.int32, (HD, lanes), 1) // group
    lane = lax.broadcasted_iota(jnp.int32, (1, lanes), 1) // group

    def one_group(g):
        r0 = g * many
        for h in range(group):
            by_head[g, pl.ds(h, many, stride=group), :] = queries[
                r0 : r0 + many, h * HD : (h + 1) * HD
            ].astype(jnp.float32)
        q_t = jnp.transpose(by_head[g])
        sides = jnp.concatenate(
            [jnp.where(owner == i, q_t, 0.0).astype(jnp.bfloat16) for i in range(many)], axis=0
        )
        span = jnp.zeros((1, lanes), jnp.int32)
        for i in range(many):
            span = jnp.where(lane == i, lengths[home + r0 + i], span)
        pltpu.make_async_copy(pages.at[g], pages.at[g], page_sem.at[g]).wait()
        cached = jnp.concatenate([pages[g, i] for i in range(many)], axis=1)
        scores = jnp.dot(cached, sides, preferred_element_type=jnp.float32) * scale
        fresh = [pairs[r0 + i].astype(jnp.float32) for i in range(many)]
        own = jnp.dot(
            jnp.concatenate(fresh, axis=1).astype(jnp.bfloat16),
            sides,
            preferred_element_type=jnp.float32,
        )[0:1] * scale
        valid = is_key & (position < span)
        peak = jnp.maximum(
            jnp.max(jnp.where(valid, scores, -jnp.inf), axis=0, keepdims=True), own
        )
        w = jnp.where(valid, jnp.exp(scores - peak), 0.0)
        w_own = jnp.exp(own - peak)
        total = jnp.sum(w, axis=0, keepdims=True) + w_own
        line = lax.broadcasted_iota(jnp.int32, (HD, lanes), 0)
        w = jnp.transpose(pltpu.roll(w, 1, 0)).astype(jnp.bfloat16)
        last = jnp.transpose(jnp.where(line == 0, w_own, total))
        w_own = last[:, 0:1].astype(jnp.bfloat16).astype(jnp.float32)
        total = last[:, 1:2]
        for i in range(0, many, 2):
            two = jnp.concatenate([pages[g, i], pages[g, i + 1]], axis=1)
            mixed = jnp.dot(
                w[i * group : (i + 2) * group], two, preferred_element_type=jnp.float32
            )
            for k in range(2):
                at = slice((i + k) * group, (i + k + 1) * group)
                value = mixed[k * group : (k + 1) * group, k * HD : (k + 1) * HD]
                value = (value + w_own[at] * fresh[i + k][1:2]) / total[at]
                heads[pl.ds((r0 + i + k) * group, group), :] = value

    for g in range(groups):
        one_group(g)
    attention = jnp.concatenate(
        [heads[pl.ds(h, requests, stride=group), :].astype(jnp.bfloat16) for h in range(group)],
        axis=1,
    )
    for n in range(SIDE):
        weight_copy(n).wait()
        part = jnp.dot(attention, weights[n], preferred_element_type=jnp.float32)
        part = part + jnp.where(x == n, homes[...].astype(jnp.float32), 0.0)
        part = part.astype(jnp.bfloat16)
        for t in range(SIDE):
            rows[t, :, n * width : (n + 1) * width] = part[t * block : (t + 1) * block]
    high = gains[...].astype(jnp.bfloat16).astype(jnp.float32)
    extra = jnp.concatenate([high, gains[...] - high], axis=0).astype(jnp.bfloat16)
    for s in range(SIDE):
        outs[s][:, : SIDE * width] = rows[(x + s) % SIDE]
        outs[s][:, SIDE * width :] = extra


def attend_project(table, lengths, place, query, new_kv, hidden, gain, pool, weight):
    requests, width = hidden.shape
    block = requests // SIDE
    group = width // HD
    many = GROUP_LANES // group
    groups = requests // many
    page_rows = pool.shape[1] * pool.shape[2]
    out = jax.ShapeDtypeStruct((block, SIDE * width + HD), jnp.bfloat16)
    return pl.pallas_call(
        attend_kernel,
        out_shape=[out] * SIDE,
        in_specs=[SM] + [HBM] * 8,
        out_specs=[VM] * SIDE,
        scratch_shapes=[
            pltpu.VMEM((groups, many, 2 * page_rows, HD), jnp.bfloat16),
            pltpu.VMEM((SIDE, weight.shape[0], width), jnp.bfloat16),
            pltpu.VMEM(query.shape, jnp.bfloat16),
            pltpu.VMEM(new_kv.shape, jnp.bfloat16),
            pltpu.VMEM(hidden.shape, jnp.bfloat16),
            pltpu.VMEM((group, HD), jnp.float32),
            pltpu.SMEM(table.shape, jnp.int32),
            pltpu.SMEM(lengths.shape, jnp.int32),
            pltpu.VMEM((groups, many * group, HD), jnp.float32),
            pltpu.VMEM((requests * group, HD), jnp.float32),
            pltpu.VMEM((SIDE, block, SIDE * width), jnp.bfloat16),
            pltpu.SemaphoreType.DMA((groups,)),
            pltpu.SemaphoreType.DMA((SIDE,)),
            pltpu.SemaphoreType.DMA((6,)),
        ],
        compiler_params=params(36),
        cost_estimate=cost(2 * requests * width * SIDE * width, 2 * (pool.size + weight.size)),
        name="attend_project",
    )(
        place,
        in_hbm(table),
        in_hbm(lengths),
        in_hbm(query),
        in_hbm(new_kv),
        in_hbm(hidden),
        in_hbm(gain.reshape(group, HD)),
        in_hbm(pool.reshape(pool.shape[0], page_rows, HD)),
        in_hbm(weight),
    )


def norm_kernel(place, *refs):
    parts, (normed, kept, gains) = refs[:SIDE], refs[SIDE:]
    x = place[0]
    width = kept.shape[2]
    lines = width // HD
    for s in range(SIDE):
        extra = parts[s][:, SIDE * width :].astype(jnp.float32)
        gains[(x + SIDE - s) % SIDE] = extra[:lines] + extra[lines:]
    square = 0.0
    residual = []
    for n in range(SIDE):
        at = slice(n * width, (n + 1) * width)
        value = sum(p[:, at].astype(jnp.float32) for p in parts)
        square = square + jnp.sum(value * value, axis=1, keepdims=True)
        kept[n] = value.astype(jnp.bfloat16)
        residual.append(value)
    factor = lax.rsqrt(square / (SIDE * width) + EPSILON)
    for n in range(SIDE):
        gain = gains[n]
        for j in range(lines):
            value = residual[n][:, j * HD : (j + 1) * HD] * factor * gain[j : j + 1]
            normed[:, n * width + j * HD : n * width + (j + 1) * HD] = value.astype(jnp.bfloat16)


def normalise(place, parts, width):
    block = parts[0].shape[0]
    return pl.pallas_call(
        norm_kernel,
        out_shape=[
            jax.ShapeDtypeStruct((block, SIDE * width), jnp.bfloat16),
            jax.ShapeDtypeStruct((SIDE, block, width), jnp.bfloat16),
        ],
        in_specs=[SM] + [VM] * SIDE,
        out_specs=[VM, VM],
        scratch_shapes=[pltpu.VMEM((SIDE, width // HD, HD), jnp.float32)],
        compiler_params=params(16),
        cost_estimate=cost(0, 12 * SIDE * block * width),
        name="normalise",
    )(place, *parts)


def join_kernel(*refs):
    parts, out = refs[:-1], refs[-1]
    rows = parts[0].shape[0]
    for i, part in enumerate(parts):
        out[i * rows : (i + 1) * rows] = part[...]


def join(parts):
    rows, width = parts[0].shape
    return pl.pallas_call(
        join_kernel,
        out_shape=jax.ShapeDtypeStruct((len(parts) * rows, width), parts[0].dtype),
        in_specs=[VM] * len(parts),
        out_specs=VM,
        compiler_params=params(4),
        cost_estimate=cost(0, 4 * len(parts) * rows * width),
        name="join",
    )(*parts)


def split_kernel(both, gate, up, sem):
    copies = [
        pltpu.make_async_copy(both.at[k], into, sem.at[k]) for k, into in enumerate((gate, up))
    ]
    for c in copies:
        c.start()
    for c in copies:
        c.wait()


def split(both):
    half = jax.ShapeDtypeStruct(both.shape[1:], both.dtype)
    return pl.pallas_call(
        split_kernel,
        out_shape=[half, half],
        in_specs=[HBM],
        out_specs=[VM, VM],
        scratch_shapes=[pltpu.SemaphoreType.DMA((2,))],
        compiler_params=params(4),
        name="split",
    )(in_hbm(both))


def gate_up_kernel(place, source, *refs):
    blocks, sides, outs = refs[: 2 * SIDE], refs[2 * SIDE : 4 * SIDE], refs[4 * SIDE : 4 * SIDE + 2]
    turned, weights, values, moved, sem = refs[4 * SIDE + 2 :]
    x = place[0]
    rows = blocks[0].shape[0]
    units, width = sides[0].shape
    apart = weights.shape[0] // 2
    copies = []
    for i, side in enumerate(sides):
        start = pl.multiple_of(((x + SIDE - i // 2) % SIDE) * width, width)
        into = weights.at[pl.ds((i % 2) * apart, units), pl.ds(start, width)]
        copies.append(pltpu.make_async_copy(side, into, sem.at[i]))
    for c in copies:
        c.start()
    for p in range(SIDE):
        pair = jnp.concatenate([blocks[2 * p][...], blocks[2 * p + 1][...]], axis=0)
        turned[:, 2 * p * rows : 2 * (p + 1) * rows] = jnp.transpose(pair)
    for c in copies:
        c.wait()
    both = jnp.dot(weights[...], turned[...], preferred_element_type=jnp.float32)
    value = jax.nn.silu(both[:units]) * both[apart : apart + units]
    spare = values.shape[1] - units
    value = jnp.concatenate([value, jnp.zeros((spare, value.shape[1]), jnp.float32)], axis=0)
    values[...] = jnp.transpose(value)
    slots = source.shape[0]
    block = values.shape[0] // slots
    for d in range(slots):
        moved[d : d + 1] = values[pl.ds(source[d] * block + block - 1, 1)]
    for d in range(slots):
        values[(d + 1) * block - 1 : (d + 1) * block] = moved[d : d + 1]
    half = values.shape[0] // 2
    for k in range(2):
        outs[k][...] = values[k * half : (k + 1) * half, :units].astype(jnp.bfloat16)


def gate_up_act(place, source, blocks, sides):
    rows, features = blocks[0].shape
    rows = rows * len(blocks)
    units = sides[0].shape[0]
    padded = -(-units // HD) * HD
    return pl.pallas_call(
        gate_up_kernel,
        out_shape=[jax.ShapeDtypeStruct((rows // 2, units), jnp.bfloat16)] * 2,
        in_specs=[SM, SM] + [VM] * (2 * SIDE) + [HBM] * (2 * SIDE),
        out_specs=[VM, VM],
        scratch_shapes=[
            pltpu.VMEM((features, rows), jnp.bfloat16),
            pltpu.VMEM((2 * (-(-units // 16) * 16), features), jnp.bfloat16),
            pltpu.VMEM((rows, padded), jnp.float32),
            pltpu.VMEM((source.shape[0], padded), jnp.float32),
            pltpu.SemaphoreType.DMA((2 * SIDE,)),
        ],
        compiler_params=params(24),
        cost_estimate=cost(4 * rows * features * units, 10 * units * features),
        name="gate_up_act",
    )(place, source, *blocks, *map(in_hbm, sides))


def down_kernel(base, picks, place, slot, weight, *refs):
    acts, homes, refs = refs[:SIDE], refs[SIDE], refs[SIDE + 1 :]
    theirs, outs = refs[: -len(picks)], refs[-len(picks) :]
    x = place[0]
    block = homes.shape[1]
    rows = SIDE * block
    inputs = [a[p * rows : (p + 1) * rows] for p in picks for a in acts]
    values = jnp.dot(
        jnp.concatenate(inputs, axis=0), weight[...], preferred_element_type=jnp.float32
    )
    line = lax.broadcasted_iota(jnp.int32, homes.shape[1:], 0)
    for s in range(SIDE):
        from_x = (x + SIDE - s) % SIDE
        home = homes[from_x].astype(jnp.float32)
        moves = (line == block - 1) & (from_x == SIDE - 1)
        for n, p in enumerate(picks):
            for d in range(SIDE):
                at = (n * SIDE + s) * rows + d * block
                value = values[at : at + block]
                here = base + p * SIDE + d
                adds = moves & (slot[0] == here)
                if here == 0:
                    adds = adds | jnp.logical_not(moves)
                value = value + jnp.where(adds, home, 0.0)
                if theirs:
                    value = value + theirs[n][d, from_x].astype(jnp.float32)
                outs[n][d, from_x] = value.astype(jnp.bfloat16)


def down(base, picks, place, slot, weight, acts, homes, theirs=()):
    block, width = homes.shape[1:]
    out = jax.ShapeDtypeStruct((SIDE, SIDE, block, width), jnp.bfloat16)
    return pl.pallas_call(
        lambda *refs: down_kernel(base, picks, *refs),
        out_shape=[out] * len(picks),
        in_specs=[SM, SM, VM] + [VM] * (SIDE + 1 + len(theirs)),
        out_specs=[VM] * len(picks),
        compiler_params=params(16),
        cost_estimate=cost(
            2 * len(picks) * SIDE * SIDE * block * weight.size, 2 * len(picks) * weight.size
        ),
        name="down",
    )(place, slot, weight, *acts, homes, *theirs)


def slot_sources(dest):
    z, y, c = (lax.axis_index(a) for a in REP)
    other, second, first = jnp.meshgrid(
        jnp.arange(2), jnp.arange(SIDE), jnp.arange(SIDE), indexing="ij"
    )
    core = (c + other) % 2
    slot_z = (z - jnp.where(core == 0, first, second)) % SIDE
    slot_y = (y - jnp.where(core == 0, second, first)) % SIDE
    group = ((slot_z * SIDE + slot_y) * 2 + core).reshape(-1)
    target = jnp.sum(
        jnp.where(group[:, None] == jnp.arange(dest.shape[0])[None, :], dest[None, :], 0), axis=1
    )
    hit = group[:, None] == target[None, :]
    return jnp.sum(jnp.where(hit, jnp.arange(group.shape[0])[None, :], 0), axis=1)


def add(values):
    return sum(v.astype(jnp.float32) for v in values).astype(jnp.bfloat16)


def local(
    hidden_in,
    query,
    new_kv,
    pool,
    page_table,
    lengths,
    dest,
    out_weight,
    norm_gain,
    gate_up,
    down_weight,
):
    rows_here, width = hidden_in.shape
    x = lax.axis_index("x")
    place = jnp.stack([x, lax.axis_index(REP)]).astype(jnp.int32)

    gate, up = split(jnp.transpose(gate_up, (1, 2, 0)))
    gate_1, up_3 = along_x(gate, 1), along_x(up, 3)

    source = slot_sources(dest).astype(jnp.int32)
    slots = source.shape[0]
    identity = jnp.arange(slots, dtype=jnp.int32)
    slot = jnp.sum(jnp.where(source == 0, identity, 0))[None]
    source = jnp.where(x == SIDE - 1, source, identity)

    parts = attend_project(
        page_table.T, lengths, place, query, new_kv, hidden_in, norm_gain, pool, out_weight
    )
    parts = [parts[0]] + [along_x(parts[s], s) for s in (1, 2, 3)]
    normed, kept = normalise(place, parts, width)
    homes = lax.all_to_all(kept, "x", 0, 0, tiled=True)
    normed, gate_1, up_3 = lax.optimization_barrier((normed, gate_1, up_3))
    gate_2, up_2 = along_x(gate_1, 1), along_x(up_3, 3)

    first = join([normed] + [along_chips(normed, s, True) for s in (1, 2, 3)])
    first, gate, up, gate_2, up_2, homes = lax.optimization_barrier(
        (first, gate, up, gate_2, up_2, homes)
    )
    gate_3, up_1 = along_x(gate, 3), along_x(up, 1)
    sides = (gate, up, gate_1, up_1, gate_2, up_2, gate_3, up_3)
    second = [first] + [along_chips(first, s, False) for s in (1, 2, 3)]
    second[0], second[1] = lax.optimization_barrier((second[0], second[1]))
    blocks = second + [other_core(v) for v in second]
    mine, theirs = gate_up_act(place, source, blocks, sides)
    mine, theirs, homes = lax.optimization_barrier((mine, theirs, homes))
    theirs_1, theirs_3 = along_x(theirs, 1), along_x(theirs, 3)
    mine_1, mine_3 = along_x(mine, 1), along_x(mine, 3)
    theirs_2 = along_x(theirs_1, 1)
    theirs_2, theirs_3, mine_1, mine_3 = lax.optimization_barrier(
        (theirs_2, theirs_3, mine_1, mine_3)
    )
    theirs = [theirs, theirs_1, theirs_2, theirs_3]
    mine = [mine, mine_1, along_x(mine_3, 3), mine_3]

    half = slots // 2
    shifts = (2, 1, 3, 0)
    pairs = ((2, 1), (3, 0))
    sent = [
        list(down(half, picks, place, slot, down_weight, theirs, homes)) for picks in pairs
    ]
    sent[1][0], mine[2] = lax.optimization_barrier((sent[1][0], mine[2]))
    received = [other_core(value) for values in sent for value in values]
    total = []
    for picks, values in (((2,), received[:1]), ((1, 3), received[1:3]), ((0,), received[3:])):
        if total:
            *values, _ = lax.optimization_barrier((*values, made[0]))
        made = down(0, picks, place, slot, down_weight, mine, homes, tuple(values))
        total += [along_chips(v, -s, False) if s else v for s, v in zip(picks, made)]
    total = add(total)
    out = add([along_chips(total[s], -s, True) for s in (2, 1, 3)] + [total[0]])
    return out.reshape(rows_here, width)


def solution(mesh):
    chips = Mesh(mesh.devices.reshape(SIDE, SIDE, 2, SIDE), ("z", "y", "c", "x"))
    return jax.shard_map(
        local,
        mesh=chips,
        in_specs=(
            P(REP, "x"),
            P(REP, "x"),
            P(REP, None, "x"),
            P(REP, None, None, "x"),
            P(REP, None),
            P(),
            P(),
            P("x", None),
            P("x"),
            P("x", None, REP),
            P(REP, "x"),
        ),
        out_specs=P(REP, "x"),
        check_vma=False,
    )
```
